128 devices in a mesh: group: 16 (over y, z), block: 8 (over x, core).
Axes of the slice: x: 4, y: 4, z: 4, core: 2. Of those that a mesh axis runs over, the one named last changes fastest.
Arguments:
- solution: float32 [16, 64, 5, 16, 256], P('group', 'block'), as said below
- register: float32 [16, 64, 5, 16, 256], P('group', 'block'), may hold values from -1.5 to 1.5
- counts: int32 [8], replicated, may hold values from 1 to 8, 32 in all
Outputs:
- new_solution: float32 [16, 64, 5, 16, 256], P('group', 'block')
- new_register: float32 [16, 64, 5, 16, 256], P('group', 'block')
The draws below stay inside these ranges and needn't reach their ends.
Inputs may be any that keep to these rules, and one draw needn't show every extreme that they name: `counts`: every index owns at least one block, and some index owns exactly 8 blocks; none owns more. `solution`: each cell in every slot, used or not, holds the conserved variables of a gas state with density between 0.5 and 2 and pressure between 0.5 and 1, with ratio of specific heats 1.4.
All inputs are finite; a program needn't handle non-finite values.
Results may differ from the reference program's by a relative error of at most 0.0003.
Values sent between devices are 32-bit elements; how exact they have to be, the bound alone decides.
A program may use at most 128 MiB of HBM per device.

```python
import math
import jax
import jax.numpy as jnp
import numpy as np
from jax import lax

BS = 16
SECTION = 2
CAP = 8
GROUPS = 16
OWNERS = 8
BPG = 32
SHEAR = 4


def draw_solution(key, part):
    shape = (GROUPS, OWNERS * CAP, BS, BS * BS)
    keys = jax.random.split(jax.random.fold_in(key, 17), 4)
    density = jnp.exp(jax.random.uniform(keys[0], shape, jnp.float32, jnp.log(0.5), jnp.log(2.0)))
    pressure = jax.random.uniform(keys[1], shape, jnp.float32, 0.5, 1.0)
    device_rank = (jnp.arange(GROUPS)[:, None] * OWNERS + jnp.arange(OWNERS * CAP)[None, :] // CAP).astype(jnp.float32)
    ramp = device_rank / (GROUPS * OWNERS - 1.0)
    amplitude = 0.5 * (1.0 + 3.0 * ramp)
    factor = jax.random.uniform(keys[2], (GROUPS, OWNERS * CAP), jnp.float32, 0.7, 1.0)
    amplitude = (amplitude * factor)[:, :, None, None]
    velocity = jax.random.uniform(keys[3], (3,) + shape, jnp.float32, -1.0, 1.0) * amplitude[None]
    energy = pressure / 0.4 + 0.5 * density * jnp.sum(velocity * velocity, axis=0)
    return jnp.stack([density, density * velocity[0], density * velocity[1], density * velocity[2], energy], axis=2)


def shard_levels(rng, dims, cuts, least, largest):
    loudness, own = 1.0, jax.random.fold_in(rng, 6)
    for axis_at, parts in cuts:
        steps = jnp.exp(jax.random.uniform(jax.random.fold_in(own, axis_at), (parts,), jnp.float32, least / len(cuts), largest / len(cuts)))
        loudness = loudness * jnp.repeat(steps, dims[axis_at] // parts).reshape([-1 if axis == axis_at else 1 for axis in range(len(dims))])
    return loudness


def split_up(amount, total, reach, slope):
    weights = [(1 << 20) // math.isqrt(standing ** slope) + 1 for standing in range(2, amount + 1)]
    rest, given = total - reach - (amount - 1), [1] * (amount - 1)
    while rest > 0:
        candidates = [i for i in range(amount - 1) if given[i] < reach]
        whole, remaining = sum([weights[i] for i in candidates]), rest
        for i in candidates:
            more = min(reach - given[i], max(1, remaining * weights[i] // whole), rest)
            given[i] = given[i] + more
            rest = rest - more
    return np.array([reach] + given)


def uneven(rng, amount, total, limit, skew):
    if amount == 2:
        one = jax.random.randint(rng, (), max(1, total - limit), min(limit, total - 1) + 1)
        return jnp.stack([one, total - one])
    sizes = jnp.asarray(split_up(amount, total, limit, skew), jnp.int32)
    pairs = (amount - 1) // 2
    source_of, sink = sizes[1:1 + 2 * pairs:2], sizes[2:2 + 2 * pairs:2]
    room = jnp.minimum(source_of - 1, limit - sink)
    moved = jax.random.randint(jax.random.fold_in(rng, 1), (pairs,), 0, 1 << 20) % (room + 1)
    sizes = sizes.at[1:1 + 2 * pairs:2].set(source_of - moved).at[2:2 + 2 * pairs:2].set(sink + moved)
    return sizes[jax.random.permutation(jax.random.fold_in(rng, 2), amount)]


def centred(own_key, shape, deviation, limit, shards=(), kind=jnp.bfloat16):
    loudness = shard_levels(own_key, shape, shards, -0.22, 0.18) if shards else 1.0
    values = jax.random.normal(own_key, shape, jnp.float32) * deviation * loudness
    return jnp.minimum(jnp.maximum(values, -limit), limit).astype(kind)


def setup_inputs(seed: int = 0) -> dict:
    key_list = jax.random.split(jax.random.key(seed), 4)
    solution = draw_solution(jax.random.fold_in(key_list[3], 71), 0)
    register = centred(key_list[1], (GROUPS, OWNERS * CAP, 5, BS, BS * BS), 0.3, 1.5, ((0, 16), (1, 8)), jnp.float32)
    counts = uneven(key_list[2], OWNERS, BPG, CAP, 2).astype(jnp.int32)
    return {"solution": solution, "register": register, "counts": counts}


HEAT_RATIO = 1.4
COURANT = 0.5
SERIES_CUT = 0.0001
CENTRAL_WEIGHTS = (0.8, -0.2, 4.0 / 105.0, -1.0 / 280.0)
LOW_STORAGE_A = (0.0, -567301805773.0 / 1357537059087.0, -2404267990393.0 / 2016746695238.0, -3550918686646.0 / 2091501179385.0, -1275806237668.0 / 842570457699.0)
LOW_STORAGE_B = (1432997174477.0 / 9575080441755.0, 5161836677717.0 / 13612068292357.0, 1720146321549.0 / 2090206949498.0, 3134564353537.0 / 4481467310338.0, 2277821191437.0 / 14882151754819.0)

def primitives(conserved):
    density = conserved[:, 0]
    velocity = conserved[:, 1:4] / density[:, None]
    pressure = (HEAT_RATIO - 1.0) * (conserved[:, 4] - 0.5 * lax.optimization_barrier(jnp.sum(conserved[:, 1:4] * velocity, axis=1)))
    return jnp.concatenate([density[:, None], velocity, pressure[:, None], jnp.log(density)[:, None], jnp.log(pressure)[:, None]], axis=1)

def wave_speed(primitive):
    speed_sq = primitive[:, 1] * primitive[:, 1] + primitive[:, 2] * primitive[:, 2] + primitive[:, 3] * primitive[:, 3]
    return jnp.sqrt(speed_sq) + jnp.sqrt(HEAT_RATIO * primitive[:, 4] / primitive[:, 0])

def squared_ratio_of(first_value, second_value):
    return (first_value * (first_value - 2.0 * second_value) + second_value * second_value) / (first_value * (first_value + 2.0 * second_value) + second_value * second_value)

def log_mean(first_value, second_value, first_log, second_log):
    ratio_sq = squared_ratio_of(first_value, second_value)
    near_equal = ratio_sq < SERIES_CUT
    series = (first_value + second_value) / (2.0 + ratio_sq * (2.0 / 3.0 + ratio_sq * (2.0 / 5.0 + ratio_sq * (2.0 / 7.0))))
    spread = jnp.where(near_equal, 1.0, second_log - first_log)
    return jnp.where(near_equal, series, (second_value - first_value) / spread)

def inverse_log_mean(first_value, second_value, first_log, second_log):
    ratio_sq = squared_ratio_of(first_value, second_value)
    near_equal = ratio_sq < SERIES_CUT
    series = (2.0 + ratio_sq * (2.0 / 3.0 + ratio_sq * (2.0 / 5.0 + ratio_sq * (2.0 / 7.0)))) / (first_value + second_value)
    spread = jnp.where(near_equal, 1.0, second_value - first_value)
    return jnp.where(near_equal, series, (second_log - first_log) / spread)

def pair_flux(left_side, right_side, direction):
    pressure_left = left_side[:, 4]
    pressure_right = right_side[:, 4]
    density_mean = log_mean(left_side[:, 0], right_side[:, 0], left_side[:, 5], right_side[:, 5])
    inverse_mean = inverse_log_mean(left_side[:, 0] * pressure_right, right_side[:, 0] * pressure_left, left_side[:, 5] + right_side[:, 6], right_side[:, 5] + left_side[:, 6])
    averages = [0.5 * (left_side[:, 1 + index] + right_side[:, 1 + index]) for index in range(3)]
    squares = 0.5 * (left_side[:, 1] * right_side[:, 1] + left_side[:, 2] * right_side[:, 2] + left_side[:, 3] * right_side[:, 3])
    pressure_mean = 0.5 * (pressure_left + pressure_right)
    mass_flux = density_mean * averages[direction]
    momenta = []
    for index in range(3):
        if index == direction:
            momenta.append(mass_flux * averages[index] + pressure_mean)
        else:
            momenta.append(mass_flux * averages[index])
    energy_flux = mass_flux * (squares + pressure_left * pressure_right * inverse_mean / (HEAT_RATIO - 1.0)) + 0.5 * (pressure_left * right_side[:, 1 + direction] + pressure_right * left_side[:, 1 + direction])
    return jnp.stack([mass_flux] + momenta + [energy_flux], axis=1)

def face_planes(fields_in):
    count, width, edge = (fields_in.shape[0], fields_in.shape[1], fields_in.shape[2])
    cubed = fields_in.reshape(count, width, edge, edge, edge)
    pieces = (cubed[:, :, :4], cubed[:, :, edge - 4:], cubed[:, :, :, :4], cubed[:, :, :, edge - 4:], cubed[..., :4], cubed[..., edge - 4:])
    return tuple((piece.reshape(count, width, 4 * edge * edge) for piece in pieces))

def block_tendency(primitive, x_lower, x_upper, y_lower, y_upper, z_lower, z_upper):
    count, width, edge = (primitive.shape[0], primitive.shape[1], primitive.shape[2])
    cubed = primitive.reshape(count, width, edge, edge, edge)
    ext_x = jnp.concatenate([x_lower.reshape(count, width, 4, edge * edge), primitive, x_upper.reshape(count, width, 4, edge * edge)], axis=2)
    ext_y = jnp.concatenate([y_lower.reshape(count, width, edge, 4, edge), cubed, y_upper.reshape(count, width, edge, 4, edge)], axis=3).reshape(count, width, edge, (edge + 8) * edge)
    ext_z = jnp.concatenate([z_lower.reshape(count, width, edge, edge, 4), cubed, z_upper.reshape(count, width, edge, edge, 4)], axis=4).reshape(count, width, edge, edge * (edge + 8))
    extent = edge * (edge + 8)
    summed = jnp.zeros((count, 5, edge, edge * edge), jnp.float32)
    summed_z = jnp.zeros((count, 5, edge, extent), jnp.float32)
    for offset in range(1, 5):
        factor = 2.0 * CENTRAL_WEIGHTS[offset - 1]
        pair_terms = pair_flux(ext_x[:, :, 4 - offset:edge + 4], ext_x[:, :, 4:edge + 4 + offset], 0)
        summed = summed + factor * (pair_terms[:, :, offset:] - pair_terms[:, :, :edge])
        pair_terms = pair_flux(ext_y[..., (4 - offset) * edge:(edge + 4) * edge], ext_y[..., 4 * edge:(edge + 4 + offset) * edge], 1)
        summed = summed + factor * (pair_terms[..., offset * edge:] - pair_terms[..., :edge * edge])
        pair_terms = pair_flux(ext_z[..., :extent - offset], ext_z[..., offset:], 2)
        difference = pair_terms[..., offset:extent - offset] - pair_terms[..., :extent - 2 * offset]
        summed_z = summed_z + factor * jnp.pad(difference, ((0, 0), (0, 0), (0, 0), (offset, offset)))
    interior = summed_z.reshape(count, 5, edge, edge, edge + 8)[..., 4:edge + 4].reshape(count, 5, edge, edge * edge)
    return -float(edge) * (summed + interior)

def reference(solution, register, counts):
    edge = BS
    counts_int = counts.astype(jnp.int32)
    starts = (jnp.cumsum(counts_int) - counts_int).astype(jnp.int32)
    positions = jnp.arange(BPG, dtype=jnp.int32)
    owner_of = (lax.optimization_barrier(jnp.sum((starts[None, :] <= positions[:, None]).astype(jnp.int32), axis=1)) - 1).astype(jnp.int32)
    slot_of = (owner_of * CAP + positions - jnp.take(starts, owner_of)).astype(jnp.int32)
    column_state = jnp.take(solution, slot_of, axis=1)
    column_register = jnp.take(register, slot_of, axis=1)
    primitive = primitives(column_state.reshape(GROUPS * BPG, 5, edge, edge * edge))
    fastest = jnp.max(wave_speed(primitive))
    time_step = COURANT / (edge * fastest)
    planes = [piece.reshape(GROUPS, BPG, 7, 4 * edge * edge) for piece in face_planes(primitive)]
    primitive = primitive.reshape(GROUPS, BPG, 7, edge, edge * edge)
    x_lower = jnp.roll(planes[1], SHEAR, axis=0)
    x_upper = jnp.roll(planes[0], -SHEAR, axis=0)
    y_lower = jnp.roll(planes[3], 1, axis=0)
    y_upper = jnp.roll(planes[2], -1, axis=0)
    z_lower = jnp.roll(planes[5], 1, axis=1)
    z_upper = jnp.roll(planes[4], -1, axis=1)

    def one_column(items):
        return block_tendency(*items)
    tendency = lax.map(one_column, (primitive, x_lower, x_upper, y_lower, y_upper, z_lower, z_upper))
    weight_a = LOW_STORAGE_A[SECTION]
    weight_b = LOW_STORAGE_B[SECTION]
    register_next = weight_a * column_register + time_step * tendency
    state_next = column_state + weight_b * register_next
    slot_ids = jnp.arange(CAP, dtype=jnp.int32)
    position_of = starts[:, None] + slot_ids[None, :]
    occupied = (slot_ids[None, :] < counts_int[:, None]).reshape(OWNERS * CAP)
    gather_index = jnp.where(occupied, position_of.reshape(OWNERS * CAP), 0).astype(jnp.int32)
    keep = occupied[None, :, None, None, None]
    new_solution = jnp.where(keep, jnp.take(state_next, gather_index, axis=1), 0.0)
    new_register = jnp.where(keep, jnp.take(register_next, gather_index, axis=1), 0.0)
    return (new_solution, new_register)
```

```python
import functools

import jax
import jax.numpy as jnp
from jax import lax
from jax.experimental import pallas as pl
from jax.experimental.pallas import tpu as pltpu
from jax.sharding import PartitionSpec as P

SECTION = 2
HEAT_RATIO = 1.4
COURANT = 0.5
SERIES_CUT = 0.0001
CENTRAL_WEIGHTS = (0.8, -0.2, 4.0 / 105.0, -1.0 / 280.0)
LOW_STORAGE_A = (
    0.0,
    -567301805773.0 / 1357537059087.0,
    -2404267990393.0 / 2016746695238.0,
    -3550918686646.0 / 2091501179385.0,
    -1275806237668.0 / 842570457699.0,
)
LOW_STORAGE_B = (
    1432997174477.0 / 9575080441755.0,
    5161836677717.0 / 13612068292357.0,
    1720146321549.0 / 2090206949498.0,
    3134564353537.0 / 4481467310338.0,
    2277821191437.0 / 14882151754819.0,
)
MESH = pl.DeviceIdType.MESH
EDGE = 16
CAP = 8
LANES = 128
FIELDS = 8


def cell_fields(state):
    density, first, second, third, energy = state
    inverse = 1.0 / density
    v1, v2, v3 = first * inverse, second * inverse, third * inverse
    pressure = (HEAT_RATIO - 1.0) * (energy - 0.5 * (first * v1 + second * v2 + third * v3))
    half_log = 0.5 * jnp.log(density)
    half_log_p = 0.5 * jnp.log(pressure)
    fields = [
        0.5 * density,
        0.5 * v1,
        0.5 * v2,
        0.5 * v3,
        0.5 * pressure,
        half_log,
        (HEAT_RATIO - 1.0) * (density / pressure),
        half_log - half_log_p,
    ]
    return fields, (v1, v2, v3, pressure, inverse)


def mean_parts(left, right, left_log, right_log):
    total = left + right
    step = right - left
    ratio = step / total
    ratio_sq = ratio * ratio
    near = ratio_sq < SERIES_CUT
    series = 1.0 + ratio_sq * (1.0 / 3.0 + ratio_sq * (1.0 / 5.0 + ratio_sq * (1.0 / 7.0)))
    return jnp.where(near, total, step), jnp.where(near, series, right_log - left_log)


def pair_flux(left, right, direction, factor):
    means = [left[1 + m] + right[1 + m] for m in range(3)]
    products = left[1] * right[1] + left[2] * right[2] + left[3] * right[3]
    top, bottom = mean_parts(left[0], right[0], left[5], right[5])
    top_t, bottom_t = mean_parts(left[6], right[6], left[7], right[7])
    mass = (top / bottom) * (factor * means[direction])
    inverse_mean = bottom_t / top_t
    momenta = [mass * means[m] for m in range(3)]
    momenta[direction] = momenta[direction] + factor * (left[4] + right[4])
    cross = left[4] * right[1 + direction] + right[4] * left[1 + direction]
    energy = mass * (products + inverse_mean) + factor * cross
    return [mass] + momenta + [energy]


FACTORS = tuple(-float(EDGE) * 2.0 * weight for weight in CENTRAL_WEIGHTS)


def tendency_kernel(
    counts_ref,
    sol_hbm,
    out_ref,
    sol,
    cons,
    pack_x,
    pack_z,
    halo_x,
    halo_y,
    halo_z,
    nat,
    tra,
    line_flux,
    plane_flux,
    tend_x,
    tend_t,
    peak,
    peak_in,
    load_sem,
    send_sem,
    recv_sem,
    peak_send,
    peak_recv,
):
    g = lax.axis_index("group")
    b = lax.axis_index("block")
    groups = lax.axis_size("group")
    owners = lax.axis_size("block")
    shear = groups // 4
    zdim = groups // shear
    base = (g // zdim) * zdim
    block_peers = [(g, lax.rem(b + j, owners)) for j in range(1, owners)]
    y_peers = [(lax.rem(g + shear * j, groups), b) for j in range(1, 4)]
    z_peers = [(base + lax.rem(g - base + j, zdim), b) for j in range(1, zdim)]
    up_y, down_y = (lax.rem(g + 1, groups), b), (lax.rem(g + groups - 1, groups), b)
    up_x, down_x = y_peers[0], y_peers[2]
    up_z, down_z = block_peers[0], block_peers[-1]

    load = pltpu.make_async_copy(sol_hbm, sol, load_sem)
    load.start()
    barrier = pltpu.get_barrier_semaphore()
    everyone = block_peers + y_peers + z_peers + [up_y, down_y]
    for peer in everyone:
        pl.semaphore_signal(barrier, inc=1, device_id=peer, device_id_type=MESH)
    load.wait()

    for f in range(5):
        for s in range(CAP):
            pack_x[0, f, 4 * s : 4 * s + 4, :] = sol[s, f, 0:4, :]
            pack_x[1, f, 4 * s : 4 * s + 4, :] = sol[s, f, EDGE - 4 : EDGE, :]
    for f in range(5):
        for half in range(2):
            part = sol[:, f, :, half * LANES : (half + 1) * LANES].reshape(LANES, LANES)
            cons[f, half * 8 : (half + 1) * 8, :, :] = part.T.reshape(8, EDGE, LANES)
    for f in range(5):
        for y in range(EDGE):
            pack_z[0, f, 4 * y : 4 * y + 4, :] = cons[f, y, 0:4, :]
            pack_z[1, f, 4 * y : 4 * y + 4, :] = cons[f, y, EDGE - 4 : EDGE, :]

    pl.semaphore_wait(barrier, len(everyone))

    def send(index, source, target, peer):
        copy = pltpu.make_async_remote_copy(
            src_ref=source,
            dst_ref=target,
            send_sem=send_sem.at[index],
            recv_sem=recv_sem.at[index],
            device_id=peer,
            device_id_type=MESH,
        )
        copy.start()
        return copy

    copies = [
        send(0, pack_z.at[1], halo_z.at[0], up_z),
        send(1, pack_z.at[0], halo_z.at[1], down_z),
        send(2, pack_x.at[1], halo_x.at[0], up_x),
        send(3, pack_x.at[0], halo_x.at[1], down_x),
        send(4, cons.at[:, EDGE - 4 : EDGE], halo_y.at[0], up_y),
        send(5, cons.at[:, 0:4], halo_y.at[1], down_y),
    ]

    owned = counts_ref[b]
    owned_below = counts_ref[lax.rem(b + owners - 1, owners)]
    lane_slot = lax.broadcasted_iota(jnp.int32, (8, LANES), 1) // EDGE

    def transposed_fields(y, fastest):
        for zt in range(2):
            rows = slice(8 * zt, 8 * zt + 8)
            fields, (v1, v2, v3, pressure, inverse) = cell_fields(
                [cons[f, y, rows, :] for f in range(5)]
            )
            for f in range(FIELDS):
                tra[f, y + 4, 8 + 8 * zt : 16 + 8 * zt, :] = fields[f]
            speed = jnp.sqrt(v1 * v1 + v2 * v2 + v3 * v3) + jnp.sqrt(
                HEAT_RATIO * pressure * inverse
            )
            fastest = jnp.maximum(fastest, speed)
        return fastest

    fastest = lax.fori_loop(0, EDGE, transposed_fields, jnp.zeros((8, LANES), jnp.float32))
    peak[0] = jnp.where(lane_slot < owned, fastest, 0.0)

    def natural_fields(s, carry):
        for half in range(2):
            for rt in range(2):
                fields, _ = cell_fields(
                    [
                        sol[s, f, 8 * rt : 8 * rt + 8, half * LANES : (half + 1) * LANES]
                        for f in range(5)
                    ]
                )
                for f in range(FIELDS):
                    nat[f, 2 * s + half, 8 + 8 * rt : 16 + 8 * rt, :] = fields[f]
        return carry

    lax.fori_loop(0, CAP, natural_fields, 0)

    def exchange_peaks(stage, first, peers):
        started = []
        for j, peer in enumerate(peers):
            copy = pltpu.make_async_remote_copy(
                src_ref=peak.at[stage],
                dst_ref=peak_in.at[first + j],
                send_sem=peak_send.at[first + j],
                recv_sem=peak_recv.at[first + j],
                device_id=peer,
                device_id_type=MESH,
            )
            copy.start()
            started.append(copy)
        return started

    def gather_peaks(stage, first, started):
        value = peak[stage]
        for j, copy in enumerate(started):
            copy.wait()
            value = jnp.maximum(value, peak_in[first + j])
        return value

    block_copies = exchange_peaks(0, 0, block_peers)

    def line_tendency(ref, line, direction, store):
        left = [
            [ref[f, line, 8 + 8 * c : 16 + 8 * c, :] for f in range(FIELDS)] for c in range(2)
        ]
        low = [ref[f, line, 4:8, :] for f in range(FIELDS)]
        total = [[None] * 5 for c in range(2)]
        for k in range(1, 5):
            below = pair_flux(
                low, [ref[f, line, 4 + k : 8 + k, :] for f in range(FIELDS)], direction, FACTORS[k - 1]
            )
            for f in range(5):
                line_flux[k - 1, f, 4:8, :] = below[f]
            for c in range(2):
                at = 8 + 8 * c
                flux = pair_flux(
                    left[c],
                    [ref[f, line, at + k : at + 8 + k, :] for f in range(FIELDS)],
                    direction,
                    FACTORS[k - 1],
                )
                for f in range(5):
                    line_flux[k - 1, f, at : at + 8, :] = flux[f]
                    total[c][f] = flux[f] if k == 1 else total[c][f] + flux[f]
            for c in range(2):
                at = 8 + 8 * c
                for f in range(5):
                    total[c][f] = total[c][f] - line_flux[k - 1, f, at - k : at + 8 - k, :]
        for c in range(2):
            for f in range(5):
                store(f, c, total[c][f])

    copies[0].wait_recv()
    copies[1].wait_recv()

    def third_halo(i, carry):
        rows = pl.ds(pl.multiple_of(8 * i, 8), 8)
        lower, upper = [], []
        for f in range(5):
            below = jnp.where(lane_slot == owned_below - 1, halo_z[0, f, rows, :], 0.0)
            above = jnp.where(lane_slot == 0, halo_z[1, f, rows, :], 0.0)
            for shift in (16, 32, 64):
                below = below + pltpu.roll(below, shift, 1)
                above = above + pltpu.roll(above, shift, 1)
            lower.append(
                jnp.where(lane_slot == 0, below, pltpu.roll(pack_z[1, f, rows, :], EDGE, 1))
            )
            upper.append(
                jnp.where(
                    lane_slot == owned - 1, above, pltpu.roll(pack_z[0, f, rows, :], LANES - EDGE, 1)
                )
            )
        lower, _ = cell_fields(lower)
        upper, _ = cell_fields(upper)
        for f in range(FIELDS):
            for j in range(2):
                tra[f, 2 * i + j + 4, 4:8, :] = lower[f][4 * j : 4 * j + 4]
                tra[f, 2 * i + j + 4, 24:28, :] = upper[f][4 * j : 4 * j + 4]
        return carry

    lax.fori_loop(0, EDGE // 2, third_halo, 0)

    def third_line(y, carry):
        def store(f, c, value):
            tend_t[f, y, 8 * c : 8 * c + 8, :] = value

        line_tendency(tra, y + 4, 2, store)
        return carry

    lax.fori_loop(0, EDGE, third_line, 0)

    peak[1] = gather_peaks(0, 0, block_copies)
    y_copies = exchange_peaks(1, owners - 1, y_peers)

    def plane_pair(y, k, zt):
        rows = slice(8 + 8 * zt, 16 + 8 * zt)
        return pair_flux(
            [tra[f, y + 4, rows, :] for f in range(FIELDS)],
            [tra[f, y + 4 + k, rows, :] for f in range(FIELDS)],
            1,
            FACTORS[k - 1],
        )

    def ahead(y, offsets):
        for zt in range(2):
            rows = slice(8 * zt, 8 * zt + 8)
            total = [tend_t[f, y, rows, :] for f in range(5)]
            for k in offsets:
                flux = plane_pair(y, k, zt)
                for f in range(5):
                    plane_flux[k - 1, f, y + 4, rows, :] = flux[f]
                    total[f] = total[f] + flux[f]
            for f in range(5):
                tend_t[f, y, rows, :] = total[f]

    def second_interior(y, carry):
        ahead(y, range(1, 5))
        return carry

    lax.fori_loop(0, EDGE - 4, second_interior, 0)
    for y in range(EDGE - 4, EDGE - 1):
        ahead(y, range(1, EDGE - y))

    copies[2].wait_recv()
    copies[3].wait_recv()

    def first_halo(i, carry):
        rows = pl.ds(pl.multiple_of(8 * i, 8), 8)
        for side in range(2):
            at = 4 if side == 0 else 24
            for half in range(2):
                lanes = slice(half * LANES, (half + 1) * LANES)
                fields, _ = cell_fields([halo_x[side, f, rows, lanes] for f in range(5)])
                for f in range(FIELDS):
                    for j in range(2):
                        nat[f, 2 * (2 * i + j) + half, at : at + 4, :] = fields[f][4 * j : 4 * j + 4]
        return carry

    lax.fori_loop(0, CAP // 2, first_halo, 0)

    def first_line(line, carry):
        def store(f, c, value):
            tend_x[f, line, 8 * c : 8 * c + 8, :] = value

        line_tendency(nat, line, 0, store)
        return carry

    lax.fori_loop(0, 2 * CAP, first_line, 0)

    peak[2] = gather_peaks(1, owners - 1, y_copies)
    z_copies = exchange_peaks(2, owners + 2, z_peers)

    copies[4].wait_recv()
    copies[5].wait_recv()

    def second_halo(y, carry):
        for side in range(2):
            for zt in range(2):
                rows = slice(8 * zt, 8 * zt + 8)
                fields, _ = cell_fields([halo_y[side, f, y, rows, :] for f in range(5)])
                for f in range(FIELDS):
                    tra[f, y + 20 * side, 8 + 8 * zt : 16 + 8 * zt, :] = fields[f]
        return carry

    lax.fori_loop(0, 4, second_halo, 0)
    for y in range(-4, 0):
        for k in range(-y, 5):
            for zt in range(2):
                flux = plane_pair(y, k, zt)
                for f in range(5):
                    plane_flux[k - 1, f, y + 4, 8 * zt : 8 * zt + 8, :] = flux[f]
    for y in range(EDGE - 4, EDGE):
        ahead(y, range(EDGE - y, 5))

    def behind(y, carry):
        for zt in range(2):
            rows = slice(8 * zt, 8 * zt + 8)
            for f in range(5):
                total = tend_t[f, y, rows, :]
                for k in range(1, 5):
                    total = total - plane_flux[k - 1, f, y + 4 - k, rows, :]
                tend_t[f, y, rows, :] = total
        return carry

    lax.fori_loop(0, EDGE, behind, 0)

    top = jnp.max(gather_peaks(2, owners + 2, z_copies), keepdims=True)
    time_step = COURANT / (EDGE * top)
    for f in range(5):
        scale = 2.0 * time_step if f == 4 else time_step
        for half in range(2):
            part = tend_t[f, half * 8 : (half + 1) * 8, :, :].reshape(LANES, LANES).T
            for s in range(CAP):
                out_ref[s, f, :, half * LANES : (half + 1) * LANES] = scale * (
                    part[s * EDGE : (s + 1) * EDGE] + tend_x[f, 2 * s + half, :, :]
                )
    for copy in copies:
        copy.wait_send()


def update_kernel(counts_ref, step_ref, sol_ref, reg_ref, new_sol_ref, new_reg_ref):
    owned = counts_ref[lax.axis_index("block")]
    size = step_ref.shape[0]
    first = pl.program_id(0) * size
    for s in range(size):
        keep = first + s < owned
        register = LOW_STORAGE_A[SECTION] * reg_ref[s] + step_ref[s]
        state = sol_ref[s] + LOW_STORAGE_B[SECTION] * register
        new_reg_ref[s] = jnp.where(keep, register, 0.0)
        new_sol_ref[s] = jnp.where(keep, state, 0.0)


def on_device(solution, register, counts):
    blocks, old_register = solution[0], register[0]
    shape = blocks.shape
    f32 = jnp.float32
    scratch = [
        pltpu.VMEM(shape, f32),
        pltpu.VMEM((5, EDGE, EDGE, LANES), f32),
        pltpu.VMEM((2, 5, 4 * CAP, 2 * LANES), f32),
        pltpu.VMEM((2, 5, 4 * EDGE, LANES), f32),
        pltpu.VMEM((2, 5, 4 * CAP, 2 * LANES), f32),
        pltpu.VMEM((2, 5, 4, EDGE, LANES), f32),
        pltpu.VMEM((2, 5, 4 * EDGE, LANES), f32),
        pltpu.VMEM((FIELDS, 2 * CAP, 32, LANES), f32),
        pltpu.VMEM((FIELDS, EDGE + 8, 32, LANES), f32),
        pltpu.VMEM((4, 5, 24, LANES), f32),
        pltpu.VMEM((4, 5, EDGE + 4, EDGE, LANES), f32),
        pltpu.VMEM((5, 2 * CAP, EDGE, LANES), f32),
        pltpu.VMEM((5, EDGE, EDGE, LANES), f32),
        pltpu.VMEM((3, 8, LANES), f32),
        pltpu.VMEM((13, 8, LANES), f32),
        pltpu.SemaphoreType.DMA,
        pltpu.SemaphoreType.DMA((6,)),
        pltpu.SemaphoreType.DMA((6,)),
        pltpu.SemaphoreType.DMA((13,)),
        pltpu.SemaphoreType.DMA((13,)),
    ]
    step = pl.pallas_call(
        tendency_kernel,
        out_shape=jax.ShapeDtypeStruct(shape, f32),
        in_specs=[
            pl.BlockSpec(memory_space=pltpu.SMEM),
            pl.BlockSpec(memory_space=pl.ANY),
        ],
        out_specs=pl.BlockSpec(memory_space=pltpu.VMEM),
        scratch_shapes=scratch,
        compiler_params=pltpu.CompilerParams(
            collective_id=0, has_side_effects=True, vmem_limit_bytes=40 * 2**20
        ),
        name="tendency",
    )(counts, blocks)
    size = 2
    spec = pl.BlockSpec((size,) + shape[1:], lambda i: (i, 0, 0, 0))
    new_solution, new_register = pl.pallas_call(
        update_kernel,
        grid=(CAP // size,),
        out_shape=[jax.ShapeDtypeStruct(shape, f32)] * 2,
        in_specs=[pl.BlockSpec(memory_space=pltpu.SMEM), spec, spec, spec],
        out_specs=[spec, spec],
        name="update",
    )(counts, step, blocks, old_register)
    return (new_solution[None], new_register[None])


def solution(mesh):
    in_specs = (P("group", "block", None, None, None), P("group", "block", None, None, None), P())
    out_specs = (P("group", "block", None, None, None), P("group", "block", None, None, None))
    return jax.shard_map(
        on_device, mesh=mesh, in_specs=in_specs, out_specs=out_specs, check_vma=False
    )
```

```python
import functools

import jax
import jax.numpy as jnp
from jax import lax
from jax.experimental import pallas as pl
from jax.experimental.pallas import tpu as pltpu
from jax.sharding import PartitionSpec as P

SECTION = 2
HEAT_RATIO = 1.4
COURANT = 0.5
SERIES_CUT = 0.0001
CENTRAL_WEIGHTS = (0.8, -0.2, 4.0 / 105.0, -1.0 / 280.0)
LOW_STORAGE_A = (
    0.0,
    -567301805773.0 / 1357537059087.0,
    -2404267990393.0 / 2016746695238.0,
    -3550918686646.0 / 2091501179385.0,
    -1275806237668.0 / 842570457699.0,
)
LOW_STORAGE_B = (
    1432997174477.0 / 9575080441755.0,
    5161836677717.0 / 13612068292357.0,
    1720146321549.0 / 2090206949498.0,
    3134564353537.0 / 4481467310338.0,
    2277821191437.0 / 14882151754819.0,
)
MESH = pl.DeviceIdType.MESH
EDGE = 16
CAP = 8
OWNERS = 8
LANES = 128
FIELDS = 8


def cell_fields(state):
    density, first, second, third, energy = state
    inverse = 1.0 / density
    v1, v2, v3 = first * inverse, second * inverse, third * inverse
    pressure = (HEAT_RATIO - 1.0) * (energy - 0.5 * (first * v1 + second * v2 + third * v3))
    half_log = 0.5 * jnp.log(density)
    half_log_p = 0.5 * jnp.log(pressure)
    fields = [
        0.5 * density,
        0.5 * v1,
        0.5 * v2,
        0.5 * v3,
        0.5 * pressure,
        half_log,
        (HEAT_RATIO - 1.0) * (density / pressure),
        half_log - half_log_p,
    ]
    return fields, (v1, v2, v3, pressure, inverse)


def mean_parts(left, right, left_log, right_log):
    total = left + right
    step = right - left
    ratio = step / total
    ratio_sq = ratio * ratio
    near = ratio_sq < SERIES_CUT
    series = 1.0 + ratio_sq * (1.0 / 3.0 + ratio_sq * (1.0 / 5.0 + ratio_sq * (1.0 / 7.0)))
    return jnp.where(near, total, step), jnp.where(near, series, right_log - left_log)


def pair_flux(left, right, direction, factor):
    means = [left[1 + m] + right[1 + m] for m in range(3)]
    products = left[1] * right[1] + left[2] * right[2] + left[3] * right[3]
    top, bottom = mean_parts(left[0], right[0], left[5], right[5])
    top_t, bottom_t = mean_parts(left[6], right[6], left[7], right[7])
    mass = (top / bottom) * (factor * means[direction])
    inverse_mean = bottom_t / top_t
    momenta = [mass * means[m] for m in range(3)]
    momenta[direction] = momenta[direction] + factor * (left[4] + right[4])
    cross = left[4] * right[1 + direction] + right[4] * left[1 + direction]
    energy = mass * (products + inverse_mean) + factor * cross
    return [mass] + momenta + [energy]


FACTORS = tuple(-float(EDGE) * 2.0 * weight for weight in CENTRAL_WEIGHTS)


def tendency_kernel(
    counts_hbm,
    sol_hbm,
    reg_hbm,
    out_ref,
    info_ref,
    sol,
    reg,
    counts_ref,
    cons,
    pack_x,
    pack_z,
    halo_x,
    halo_y,
    halo_z,
    nat,
    tra,
    line_flux,
    plane_flux,
    tend_x,
    tend_t,
    peak,
    peak_in,
    load_sem,
    counts_sem,
    reg_sem,
    send_sem,
    recv_sem,
    peak_send,
    peak_recv,
):
    g = lax.axis_index("group")
    b = lax.axis_index("block")
    groups = lax.axis_size("group")
    owners = lax.axis_size("block")
    shear = groups // 4
    zdim = groups // shear
    base = (g // zdim) * zdim
    block_peers = [(g, lax.rem(b + j, owners)) for j in range(1, owners)]
    y_peers = [(lax.rem(g + shear * j, groups), b) for j in range(1, 4)]
    z_peers = [(base + lax.rem(g - base + j, zdim), b) for j in range(1, zdim)]
    up_y, down_y = (lax.rem(g + 1, groups), b), (lax.rem(g + groups - 1, groups), b)
    up_x, down_x = y_peers[0], y_peers[2]
    up_z, down_z = block_peers[0], block_peers[-1]

    counts_load = pltpu.make_async_copy(counts_hbm, counts_ref, counts_sem)
    counts_load.start()
    load = pltpu.make_async_copy(sol_hbm, sol, load_sem)
    load.start()
    barrier = pltpu.get_barrier_semaphore()
    everyone = [up_y, down_y] + y_peers + z_peers + block_peers
    for peer in everyone:
        pl.semaphore_signal(barrier, inc=1, device_id=peer, device_id_type=MESH)
    reg_load = pltpu.make_async_copy(reg_hbm, reg, reg_sem)
    reg_load.start()
    counts_load.wait()
    owned = counts_ref[b]
    owned_below = counts_ref[lax.rem(b + owners - 1, owners)]
    lane_slot = lax.broadcasted_iota(jnp.int32, (8, LANES), 1) // EDGE
    load.wait()

    def natural_fields(s, fastest):
        used = jnp.full((8, LANES), s, jnp.int32) < owned
        for half in range(2):
            for rt in range(2):
                fields, (v1, v2, v3, pressure, inverse) = cell_fields(
                    [
                        sol[s, f, 8 * rt : 8 * rt + 8, half * LANES : (half + 1) * LANES]
                        for f in range(5)
                    ]
                )
                for f in range(FIELDS):
                    nat[f, 2 * s + half, 8 + 8 * rt : 16 + 8 * rt, :] = fields[f]
                speed = jnp.sqrt(v1 * v1 + v2 * v2 + v3 * v3) + jnp.sqrt(
                    HEAT_RATIO * pressure * inverse
                )
                fastest = jnp.maximum(fastest, jnp.where(used, speed, 0.0))
        return fastest

    peak[0] = lax.fori_loop(0, CAP, natural_fields, jnp.zeros((8, LANES), jnp.float32))

    for f in range(5):
        for s in range(CAP):
            pack_x[0, f, 4 * s : 4 * s + 4, :] = sol[s, f, 0:4, :]
            pack_x[1, f, 4 * s : 4 * s + 4, :] = sol[s, f, EDGE - 4 : EDGE, :]
    for f in range(5):
        for half in range(2):
            part = sol[:, f, :, half * LANES : (half + 1) * LANES].reshape(LANES, LANES)
            cons[f, half * 8 : (half + 1) * 8, :, :] = part.T.reshape(8, EDGE, LANES)
    for f in range(5):
        for y in range(EDGE):
            pack_z[0, f, 4 * y : 4 * y + 4, :] = cons[f, y, 0:4, :]
            pack_z[1, f, 4 * y : 4 * y + 4, :] = cons[f, y, EDGE - 4 : EDGE, :]

    def exchange_peaks(stage, first, peers):
        started = []
        for j, peer in enumerate(peers):
            copy = pltpu.make_async_remote_copy(
                src_ref=peak.at[stage],
                dst_ref=peak_in.at[first + j],
                send_sem=peak_send.at[first + j],
                recv_sem=peak_recv.at[first + j],
                device_id=peer,
                device_id_type=MESH,
            )
            copy.start()
            started.append(copy)
        return started

    def gather_peaks(stage, first, started):
        value = peak[stage]
        for j, copy in enumerate(started):
            copy.wait()
            value = jnp.maximum(value, peak_in[first + j])
        return value

    pl.semaphore_wait(barrier, len(everyone))
    block_copies = exchange_peaks(0, 0, block_peers)

    def send(index, source, target, peer):
        copy = pltpu.make_async_remote_copy(
            src_ref=source,
            dst_ref=target,
            send_sem=send_sem.at[index],
            recv_sem=recv_sem.at[index],
            device_id=peer,
            device_id_type=MESH,
        )
        copy.start()
        return copy

    copies = [
        send(0, pack_z.at[1], halo_z.at[0], up_z),
        send(1, pack_z.at[0], halo_z.at[1], down_z),
        send(2, pack_x.at[1], halo_x.at[0], up_x),
        send(3, pack_x.at[0], halo_x.at[1], down_x),
        send(4, cons.at[:, EDGE - 4 : EDGE], halo_y.at[0], up_y),
        send(5, cons.at[:, 0:4], halo_y.at[1], down_y),
    ]

    def transposed_fields(y, carry):
        for zt in range(2):
            rows = slice(8 * zt, 8 * zt + 8)
            fields = cell_fields([cons[f, y, rows, :] for f in range(5)])[0]
            for f in range(FIELDS):
                tra[f, y + 4, 8 + 8 * zt : 16 + 8 * zt, :] = fields[f]
        return carry

    lax.fori_loop(0, EDGE, transposed_fields, 0)


    def line_tendency(ref, line, direction, store):
        left = [
            [ref[f, line, 8 + 8 * c : 16 + 8 * c, :] for f in range(FIELDS)] for c in range(2)
        ]
        low = [ref[f, line, 4:8, :] for f in range(FIELDS)]
        total = [[None] * 5 for c in range(2)]
        for k in range(1, 5):
            below = pair_flux(
                low, [ref[f, line, 4 + k : 8 + k, :] for f in range(FIELDS)], direction, FACTORS[k - 1]
            )
            for f in range(5):
                line_flux[k - 1, f, 4:8, :] = below[f]
            for c in range(2):
                at = 8 + 8 * c
                flux = pair_flux(
                    left[c],
                    [ref[f, line, at + k : at + 8 + k, :] for f in range(FIELDS)],
                    direction,
                    FACTORS[k - 1],
                )
                for f in range(5):
                    line_flux[k - 1, f, at : at + 8, :] = flux[f]
                    total[c][f] = flux[f] if k == 1 else total[c][f] + flux[f]
            for c in range(2):
                at = 8 + 8 * c
                for f in range(5):
                    total[c][f] = total[c][f] - line_flux[k - 1, f, at - k : at + 8 - k, :]
        for c in range(2):
            for f in range(5):
                store(f, c, total[c][f])

    def plane_pair(y, k, zt):
        rows = slice(8 + 8 * zt, 16 + 8 * zt)
        return pair_flux(
            [tra[f, y + 4, rows, :] for f in range(FIELDS)],
            [tra[f, y + 4 + k, rows, :] for f in range(FIELDS)],
            1,
            FACTORS[k - 1],
        )

    def ahead(y, offsets, fresh):
        for zt in range(2):
            rows = slice(8 * zt, 8 * zt + 8)
            total = [None if fresh else tend_t[f, y, rows, :] for f in range(5)]
            for k in offsets:
                flux = plane_pair(y, k, zt)
                for f in range(5):
                    plane_flux[k - 1, f, y + 4, rows, :] = flux[f]
                    total[f] = flux[f] if total[f] is None else total[f] + flux[f]
            for f in range(5):
                tend_t[f, y, rows, :] = total[f]

    def second_interior(y, carry):
        ahead(y, range(1, 5), True)
        return carry

    lax.fori_loop(0, EDGE - 4, second_interior, 0)
    for y in range(EDGE - 4, EDGE - 1):
        ahead(y, range(1, EDGE - y), True)
    for f in range(5):
        tend_t[f, EDGE - 1, :, :] = jnp.zeros((EDGE, LANES), jnp.float32)

    copies[0].wait_recv()
    copies[1].wait_recv()

    def third_halo(i, carry):
        rows = pl.ds(pl.multiple_of(8 * i, 8), 8)
        lower, upper = [], []
        for f in range(5):
            below = jnp.where(lane_slot == owned_below - 1, halo_z[0, f, rows, :], 0.0)
            above = jnp.where(lane_slot == 0, halo_z[1, f, rows, :], 0.0)
            for shift in (16, 32, 64):
                below = below + pltpu.roll(below, shift, 1)
                above = above + pltpu.roll(above, shift, 1)
            lower.append(
                jnp.where(lane_slot == 0, below, pltpu.roll(pack_z[1, f, rows, :], EDGE, 1))
            )
            upper.append(
                jnp.where(
                    lane_slot == owned - 1, above, pltpu.roll(pack_z[0, f, rows, :], LANES - EDGE, 1)
                )
            )
        lower, _ = cell_fields(lower)
        upper, _ = cell_fields(upper)
        for f in range(FIELDS):
            for j in range(2):
                tra[f, 2 * i + j + 4, 4:8, :] = lower[f][4 * j : 4 * j + 4]
                tra[f, 2 * i + j + 4, 24:28, :] = upper[f][4 * j : 4 * j + 4]
        return carry

    lax.fori_loop(0, EDGE // 2, third_halo, 0)

    def third_line(y, carry):
        def store(f, c, value):
            rows = slice(8 * c, 8 * c + 8)
            tend_t[f, y, rows, :] = tend_t[f, y, rows, :] + value

        line_tendency(tra, y + 4, 2, store)
        return carry

    lax.fori_loop(0, EDGE // 2, third_line, 0)
    peak[1] = gather_peaks(0, 0, block_copies)
    z_copies = exchange_peaks(1, owners - 1, z_peers)
    lax.fori_loop(EDGE // 2, EDGE, third_line, 0)

    copies[2].wait_recv()
    copies[3].wait_recv()

    def first_halo(i, carry):
        rows = pl.ds(pl.multiple_of(8 * i, 8), 8)
        for side in range(2):
            at = 4 if side == 0 else 24
            for half in range(2):
                lanes = slice(half * LANES, (half + 1) * LANES)
                fields, _ = cell_fields([halo_x[side, f, rows, lanes] for f in range(5)])
                for f in range(FIELDS):
                    for j in range(2):
                        nat[f, 2 * (2 * i + j) + half, at : at + 4, :] = fields[f][4 * j : 4 * j + 4]
        return carry

    lax.fori_loop(0, CAP // 2, first_halo, 0)

    def first_line(line, carry):
        def store(f, c, value):
            tend_x[f, line, 8 * c : 8 * c + 8, :] = value

        line_tendency(nat, line, 0, store)
        return carry

    lax.fori_loop(0, CAP, first_line, 0)
    peak[2] = gather_peaks(1, owners - 1, z_copies)
    y_copies = exchange_peaks(2, owners + 2, y_peers)
    lax.fori_loop(CAP, 2 * CAP, first_line, 0)

    copies[4].wait_recv()
    copies[5].wait_recv()

    def second_halo(y, carry):
        for side in range(2):
            for zt in range(2):
                rows = slice(8 * zt, 8 * zt + 8)
                fields, _ = cell_fields([halo_y[side, f, y, rows, :] for f in range(5)])
                for f in range(FIELDS):
                    tra[f, y + 20 * side, 8 + 8 * zt : 16 + 8 * zt, :] = fields[f]
        return carry

    lax.fori_loop(0, 4, second_halo, 0)
    for y in range(-4, 0):
        for k in range(-y, 5):
            for zt in range(2):
                flux = plane_pair(y, k, zt)
                for f in range(5):
                    plane_flux[k - 1, f, y + 4, 8 * zt : 8 * zt + 8, :] = flux[f]
    for y in range(EDGE - 4, EDGE):
        ahead(y, range(EDGE - y, 5), False)

    def behind(y, carry):
        for zt in range(2):
            rows = slice(8 * zt, 8 * zt + 8)
            for f in range(5):
                total = tend_t[f, y, rows, :]
                for k in range(1, 5):
                    total = total - plane_flux[k - 1, f, y + 4 - k, rows, :]
                tend_t[f, y, rows, :] = total
        return carry

    lax.fori_loop(0, EDGE, behind, 0)

    for f in range(5):
        for half in range(2):
            part = tend_t[f, half * 8 : (half + 1) * 8, :, :].reshape(LANES, LANES).T
            for s in range(CAP):
                value = part[s * EDGE : (s + 1) * EDGE] + tend_x[f, 2 * s + half, :, :]
                out_ref[s, f, :, half * LANES : (half + 1) * LANES] = (
                    2.0 * value if f == 4 else value
                )
    info_ref[1] = jnp.full((8, LANES), owned, jnp.int32).astype(jnp.float32)
    info_ref[0] = gather_peaks(2, owners + 2, y_copies)
    for copy in copies:
        copy.wait_send()
    reg_load.wait()


def update_kernel(tend_ref, info_ref, sol_ref, reg_ref, sol_hbm, reg_hbm, new_sol, new_reg, sems):
    fastest = jnp.max(info_ref[0], axis=(0, 1), keepdims=True)
    time_step = jnp.broadcast_to(COURANT / (EDGE * fastest), (EDGE, 2 * LANES))
    owned = jnp.broadcast_to(info_ref[1, 0:1, 0:1], (EDGE, 2 * LANES))
    copies = []
    for s in range(CAP):
        keep = owned > float(s)
        for f in range(5):
            register = LOW_STORAGE_A[SECTION] * reg_ref[s, f] + time_step * tend_ref[s, f]
            state = sol_ref[s, f] + LOW_STORAGE_B[SECTION] * register
            new_reg[s, f] = jnp.where(keep, register, 0.0)
            new_sol[s, f] = jnp.where(keep, state, 0.0)
        if s % 2 == 1:
            part = pl.ds(s - 1, 2)
            for i, (source, target) in enumerate(((new_reg, reg_hbm), (new_sol, sol_hbm))):
                copy = pltpu.make_async_copy(source.at[part], target.at[part], sems.at[i, s // 2])
                copy.start()
                copies.append(copy)
    for copy in copies:
        copy.wait()


def on_device(solution, register, counts):
    blocks, old_register = solution[0], register[0]
    shape = blocks.shape
    f32 = jnp.float32
    scratch = [
        pltpu.SMEM((OWNERS,), jnp.int32),
        pltpu.VMEM((5, EDGE, EDGE, LANES), f32),
        pltpu.VMEM((2, 5, 4 * CAP, 2 * LANES), f32),
        pltpu.VMEM((2, 5, 4 * EDGE, LANES), f32),
        pltpu.VMEM((2, 5, 4 * CAP, 2 * LANES), f32),
        pltpu.VMEM((2, 5, 4, EDGE, LANES), f32),
        pltpu.VMEM((2, 5, 4 * EDGE, LANES), f32),
        pltpu.VMEM((FIELDS, 2 * CAP, 32, LANES), f32),
        pltpu.VMEM((FIELDS, EDGE + 8, 32, LANES), f32),
        pltpu.VMEM((4, 5, 24, LANES), f32),
        pltpu.VMEM((4, 5, EDGE + 4, EDGE, LANES), f32),
        pltpu.VMEM((5, 2 * CAP, EDGE, LANES), f32),
        pltpu.VMEM((5, EDGE, EDGE, LANES), f32),
        pltpu.VMEM((3, 8, LANES), f32),
        pltpu.VMEM((13, 8, LANES), f32),
        pltpu.SemaphoreType.DMA,
        pltpu.SemaphoreType.DMA,
        pltpu.SemaphoreType.DMA,
        pltpu.SemaphoreType.DMA((6,)),
        pltpu.SemaphoreType.DMA((6,)),
        pltpu.SemaphoreType.DMA((13,)),
        pltpu.SemaphoreType.DMA((13,)),
    ]
    cells = jax.ShapeDtypeStruct(shape, f32)
    tendency, info, state, past = pl.pallas_call(
        tendency_kernel,
        out_shape=[cells, jax.ShapeDtypeStruct((2, 8, LANES), f32), cells, cells],
        in_specs=[pl.BlockSpec(memory_space=pltpu.HBM)] * 3,
        out_specs=[pl.BlockSpec(memory_space=pltpu.VMEM)] * 4,
        scratch_shapes=scratch,
        compiler_params=pltpu.CompilerParams(
            collective_id=0, has_side_effects=True, vmem_limit_bytes=20 * 2**20
        ),
        name="tendency",
    )(
        pltpu.with_memory_space_constraint(counts, pltpu.HBM),
        pltpu.with_memory_space_constraint(blocks, pltpu.HBM),
        pltpu.with_memory_space_constraint(old_register, pltpu.HBM),
    )
    new_solution, new_register = pl.pallas_call(
        update_kernel,
        out_shape=[jax.ShapeDtypeStruct(shape, f32)] * 2,
        in_specs=[pl.BlockSpec(memory_space=pltpu.VMEM)] * 4,
        out_specs=[pl.BlockSpec(memory_space=pltpu.HBM)] * 2,
        scratch_shapes=[
            pltpu.VMEM(shape, f32),
            pltpu.VMEM(shape, f32),
            pltpu.SemaphoreType.DMA((2, CAP // 2)),
        ],
        compiler_params=pltpu.CompilerParams(vmem_limit_bytes=8 * 2**20),
        name="update",
    )(tendency, info, state, past)
    return (new_solution[None], new_register[None])


def solution(mesh):
    in_specs = (P("group", "block", None, None, None), P("group", "block", None, None, None), P())
    out_specs = (P("group", "block", None, None, None), P("group", "block", None, None, None))
    return jax.shard_map(
        on_device, mesh=mesh, in_specs=in_specs, out_specs=out_specs, check_vma=False
    )
```

```python
import functools

import jax
import jax.numpy as jnp
from jax import lax
from jax.experimental import pallas as pl
from jax.experimental.pallas import tpu as pltpu
from jax.sharding import PartitionSpec as P

SECTION = 2
HEAT_RATIO = 1.4
COURANT = 0.5
SERIES_CUT = 0.0001
CENTRAL_WEIGHTS = (0.8, -0.2, 4.0 / 105.0, -1.0 / 280.0)
LOW_STORAGE_A = (
    0.0,
    -567301805773.0 / 1357537059087.0,
    -2404267990393.0 / 2016746695238.0,
    -3550918686646.0 / 2091501179385.0,
    -1275806237668.0 / 842570457699.0,
)
LOW_STORAGE_B = (
    1432997174477.0 / 9575080441755.0,
    5161836677717.0 / 13612068292357.0,
    1720146321549.0 / 2090206949498.0,
    3134564353537.0 / 4481467310338.0,
    2277821191437.0 / 14882151754819.0,
)
MESH = pl.DeviceIdType.MESH
EDGE = 16
CAP = 8
OWNERS = 8
LANES = 128
FIELDS = 8
INNER = 2
OUTER = 2


def cell_fields(state):
    density, first, second, third, energy = state
    inverse = 1.0 / density
    v1, v2, v3 = first * inverse, second * inverse, third * inverse
    pressure = (HEAT_RATIO - 1.0) * (energy - 0.5 * (first * v1 + second * v2 + third * v3))
    half_log = 0.5 * jnp.log(density)
    half_log_p = 0.5 * jnp.log(pressure)
    fields = [
        0.5 * density,
        0.5 * v1,
        0.5 * v2,
        0.5 * v3,
        0.5 * pressure,
        half_log,
        (HEAT_RATIO - 1.0) * (density / pressure),
        half_log - half_log_p,
    ]
    return fields, (v1, v2, v3, pressure, inverse)


def mean_parts(left, right, left_log, right_log):
    total = left + right
    step = right - left
    ratio = step / total
    ratio_sq = ratio * ratio
    near = ratio_sq < SERIES_CUT
    series = 1.0 + ratio_sq * (1.0 / 3.0 + ratio_sq * (1.0 / 5.0 + ratio_sq * (1.0 / 7.0)))
    return jnp.where(near, total, step), jnp.where(near, series, right_log - left_log)


def pair_flux(left, right, direction, factor):
    means = [left[1 + m] + right[1 + m] for m in range(3)]
    products = left[1] * right[1] + left[2] * right[2] + left[3] * right[3]
    top, bottom = mean_parts(left[0], right[0], left[5], right[5])
    top_t, bottom_t = mean_parts(left[6], right[6], left[7], right[7])
    mass = (top / bottom) * (factor * means[direction])
    inverse_mean = bottom_t / top_t
    momenta = [mass * means[m] for m in range(3)]
    momenta[direction] = momenta[direction] + factor * (left[4] + right[4])
    cross = left[4] * right[1 + direction] + right[4] * left[1 + direction]
    energy = mass * (products + inverse_mean) + factor * cross
    return [mass] + momenta + [energy]


FACTORS = tuple(-float(EDGE) * 2.0 * weight for weight in CENTRAL_WEIGHTS)


def tendency_kernel(
    counts_hbm,
    sol_hbm,
    reg_hbm,
    out_ref,
    info_ref,
    sol,
    reg,
    counts_ref,
    cons,
    pack_x,
    pack_z,
    halo_x,
    halo_y,
    halo_z,
    nat,
    tra,
    line_flux,
    plane_flux,
    tend_x,
    tend_t,
    peak,
    peak_in,
    load_sem,
    counts_sem,
    reg_sem,
    send_sem,
    recv_sem,
    peak_send,
    peak_recv,
):
    g = lax.axis_index("group")
    b = lax.axis_index("block")
    groups = lax.axis_size("group")
    owners = lax.axis_size("block")
    shear = groups // 4
    zdim = groups // shear
    base = (g // zdim) * zdim
    block_peers = [(g, lax.rem(b + j, owners)) for j in range(1, owners)]
    y_peers = [(lax.rem(g + shear * j, groups), b) for j in range(1, 4)]
    z_peers = [(base + lax.rem(g - base + j, zdim), b) for j in range(1, zdim)]
    up_y, down_y = (lax.rem(g + 1, groups), b), (lax.rem(g + groups - 1, groups), b)
    up_x, down_x = y_peers[0], y_peers[2]
    up_z, down_z = block_peers[0], block_peers[-1]

    counts_load = pltpu.make_async_copy(counts_hbm, counts_ref, counts_sem)
    counts_load.start()
    loads = [pltpu.make_async_copy(sol_hbm.at[s], sol.at[s], load_sem.at[s]) for s in range(CAP)]
    for load in loads:
        load.start()
    barrier = pltpu.get_barrier_semaphore()
    everyone = [up_y, down_y] + y_peers + z_peers + block_peers
    for peer in everyone:
        pl.semaphore_signal(barrier, inc=1, device_id=peer, device_id_type=MESH)
    reg_load = pltpu.make_async_copy(reg_hbm, reg, reg_sem)
    reg_load.start()
    counts_load.wait()
    owned = counts_ref[b]
    owned_below = counts_ref[lax.rem(b + owners - 1, owners)]
    lane_slot = lax.broadcasted_iota(jnp.int32, (8, LANES), 1) // EDGE

    def natural_fields(s, fastest):
        pltpu.make_async_copy(sol_hbm.at[s], sol.at[s], load_sem.at[s]).wait()
        used = jnp.full((8, LANES), s, jnp.int32) < owned
        for half in range(2):
            for rt in range(2):
                fields, (v1, v2, v3, pressure, inverse) = cell_fields(
                    [
                        sol[s, f, 8 * rt : 8 * rt + 8, half * LANES : (half + 1) * LANES]
                        for f in range(5)
                    ]
                )
                for f in range(FIELDS):
                    nat[f, 2 * s + half, 8 + 8 * rt : 16 + 8 * rt, :] = fields[f]
                    if rt == 1:
                        nat[f, 2 * s + half, 24:32, :] = fields[f]
                speed = jnp.sqrt(v1 * v1 + v2 * v2 + v3 * v3) + jnp.sqrt(
                    HEAT_RATIO * pressure * inverse
                )
                fastest = jnp.maximum(fastest, jnp.where(used, speed, 0.0))
        return fastest

    peak[0] = lax.fori_loop(0, CAP, natural_fields, jnp.zeros((8, LANES), jnp.float32))

    for f in range(5):
        for s in range(CAP):
            pack_x[0, f, 4 * s : 4 * s + 4, :] = sol[s, f, 0:4, :]
            pack_x[1, f, 4 * s : 4 * s + 4, :] = sol[s, f, EDGE - 4 : EDGE, :]
    def exchange_peaks(stage, first, peers):
        started = []
        for j, peer in enumerate(peers):
            copy = pltpu.make_async_remote_copy(
                src_ref=peak.at[stage],
                dst_ref=peak_in.at[first + j],
                send_sem=peak_send.at[first + j],
                recv_sem=peak_recv.at[first + j],
                device_id=peer,
                device_id_type=MESH,
            )
            copy.start()
            started.append(copy)
        return started

    def gather_peaks(stage, first, started):
        value = peak[stage]
        for j, copy in enumerate(started):
            copy.wait()
            value = jnp.maximum(value, peak_in[first + j])
        return value

    pl.semaphore_wait(barrier, len(everyone))
    block_copies = exchange_peaks(0, 0, block_peers)

    def send(index, source, target, peer):
        copy = pltpu.make_async_remote_copy(
            src_ref=source,
            dst_ref=target,
            send_sem=send_sem.at[index],
            recv_sem=recv_sem.at[index],
            device_id=peer,
            device_id_type=MESH,
        )
        copy.start()
        return copy

    copies = {
        2: send(2, pack_x.at[1], halo_x.at[0], up_x),
        3: send(3, pack_x.at[0], halo_x.at[1], down_x),
    }

    for f in range(5):
        for half in range(2):
            part = sol[:, f, :, half * LANES : (half + 1) * LANES].reshape(LANES, LANES)
            cons[f, half * 8 : (half + 1) * 8, :, :] = part.T.reshape(8, EDGE, LANES)
    for f in range(5):
        for y in range(EDGE):
            pack_z[0, f, 4 * y : 4 * y + 4, :] = cons[f, y, 0:4, :]
            pack_z[1, f, 4 * y : 4 * y + 4, :] = cons[f, y, EDGE - 4 : EDGE, :]

    copies[4] = send(4, cons.at[:, EDGE - 4 : EDGE], halo_y.at[0], up_y)
    copies[5] = send(5, cons.at[:, 0:4], halo_y.at[1], down_y)
    copies[0] = send(0, pack_z.at[1], halo_z.at[0], up_z)
    copies[1] = send(1, pack_z.at[0], halo_z.at[1], down_z)

    def transposed_fields(group, carry):
        for y in [2 * group + u for u in range(2)]:
            for zt in range(2):
                rows = slice(8 * zt, 8 * zt + 8)
                fields = cell_fields([cons[f, y, rows, :] for f in range(5)])[0]
                for f in range(FIELDS):
                    tra[f, y + 4, 8 + 8 * zt : 16 + 8 * zt, :] = fields[f]
                    if zt == 1:
                        tra[f, y + 4, 24:32, :] = fields[f]
        return carry

    lax.fori_loop(0, (EDGE) // 2, transposed_fields, 0)


    row = lax.broadcasted_iota(jnp.int32, (8, LANES), 0)
    is_low = row < 4
    inner = [jnp.where(row < 8 - k, FACTORS[k - 1], 0.0) for k in range(1, 5)]
    outer = [
        jnp.where(
            is_low,
            jnp.where(row < k, -FACTORS[k - 1], 0.0),
            jnp.where(row >= 8 - k, FACTORS[k - 1], 0.0),
        )
        for k in range(1, 5)
    ]
    for u in range(2):
        for k in range(4):
            for f in range(5):
                line_flux[u, k, f, 0:8, :] = jnp.zeros((8, LANES), jnp.float32)

    def line_interior(ref, line, direction, u):
        left = [
            [ref[f, line, 8 + 8 * c : 16 + 8 * c, :] for f in range(FIELDS)] for c in range(2)
        ]
        total = [[None] * 5 for c in range(2)]
        for k in range(1, 5):
            for c in range(2):
                at = 8 + 8 * c
                flux = pair_flux(
                    left[c],
                    [ref[f, line, at + k : at + 8 + k, :] for f in range(FIELDS)],
                    direction,
                    inner[k - 1] if c == 1 else FACTORS[k - 1],
                )
                for f in range(5):
                    line_flux[u, k - 1, f, at : at + 8, :] = flux[f]
                    total[c][f] = flux[f] if k == 1 else total[c][f] + flux[f]
            for c in range(2):
                at = 8 + 8 * c
                for f in range(5):
                    total[c][f] = total[c][f] - line_flux[u, k - 1, f, at - k : at + 8 - k, :]
        return total

    def line_boundary(ref, line, direction):
        first_rows = [ref[f, line, 8:16, :] for f in range(FIELDS)]
        last_rows = [ref[f, line, 16:24, :] for f in range(FIELDS)]
        total = [None] * 5
        for k in range(1, 5):
            flux = pair_flux(
                [
                    jnp.where(is_low, ref[f, line, 8 - k : 16 - k, :], last_rows[f])
                    for f in range(FIELDS)
                ],
                [
                    jnp.where(is_low, first_rows[f], ref[f, line, 16 + k : 24 + k, :])
                    for f in range(FIELDS)
                ],
                direction,
                outer[k - 1],
            )
            for f in range(5):
                total[f] = flux[f] if k == 1 else total[f] + flux[f]
        return [jnp.where(is_low, t, 0.0) for t in total], [jnp.where(is_low, 0.0, t) for t in total]

    def plane_pair(y, k, zt):
        rows = slice(8 + 8 * zt, 16 + 8 * zt)
        return pair_flux(
            [tra[f, y + 4, rows, :] for f in range(FIELDS)],
            [tra[f, y + 4 + k, rows, :] for f in range(FIELDS)],
            1,
            FACTORS[k - 1],
        )

    def ahead(y, offsets):
        for zt in range(2):
            rows = slice(8 * zt, 8 * zt + 8)
            total = [None] * 5
            for k in offsets:
                flux = plane_pair(y, k, zt)
                for f in range(5):
                    plane_flux[k - 1, f, y + 4, rows, :] = flux[f]
                    total[f] = flux[f] if total[f] is None else total[f] + flux[f]
            for f in range(5):
                tend_t[f, y, rows, :] = total[f]

    def second_interior(y, carry):
        ahead(y, range(1, 5))
        return carry

    lax.fori_loop(0, EDGE - 4, second_interior, 0)
    for y in range(EDGE - 4, EDGE - 1):
        ahead(y, range(1, EDGE - y))
    for f in range(5):
        tend_t[f, EDGE - 1, :, :] = jnp.zeros((EDGE, LANES), jnp.float32)

    peak[1] = gather_peaks(0, 0, block_copies)
    z_copies = exchange_peaks(1, owners - 1, z_peers)

    def behind(y, offsets):
        for zt in range(2):
            rows = slice(8 * zt, 8 * zt + 8)
            for f in range(5):
                total = tend_t[f, y, rows, :]
                for k in offsets:
                    total = total - plane_flux[k - 1, f, y + 4 - k, rows, :]
                tend_t[f, y, rows, :] = total

    def second_behind(y, carry):
        behind(y, range(1, 5))
        return carry

    for y in range(1, 4):
        behind(y, range(1, y + 1))
    lax.fori_loop(4, EDGE, second_behind, 0)

    def third_line(i, carry):
        for u in range(INNER):
            y = INNER * i + u
            total = line_interior(tra, y + 4, 2, u)
            for f in range(5):
                for c in range(2):
                    rows = slice(8 * c, 8 * c + 8)
                    tend_t[f, y, rows, :] = tend_t[f, y, rows, :] + total[c][f]
        return carry

    def first_line(i, carry):
        for u in range(INNER):
            line = INNER * i + u
            total = line_interior(nat, line, 0, u)
            for f in range(5):
                for c in range(2):
                    tend_x[f, line, 8 * c : 8 * c + 8, :] = total[c][f]
        return carry

    lax.fori_loop(0, EDGE // INNER, third_line, 0)
    lax.fori_loop(0, CAP // INNER, first_line, 0)
    peak[2] = gather_peaks(1, owners - 1, z_copies)
    y_copies = exchange_peaks(2, owners + 2, y_peers)
    lax.fori_loop(CAP // INNER, 2 * CAP // INNER, first_line, 0)

    copies[0].wait_recv()
    copies[1].wait_recv()

    def third_halo(group, carry):
        for i in [4 * group + u for u in range(4)]:
            rows = pl.ds(pl.multiple_of(8 * i, 8), 8)
            lower, upper = [], []
            for f in range(5):
                below = jnp.where(lane_slot == owned_below - 1, halo_z[0, f, rows, :], 0.0)
                above = jnp.where(lane_slot == 0, halo_z[1, f, rows, :], 0.0)
                for shift in (16, 32, 64):
                    below = below + pltpu.roll(below, shift, 1)
                    above = above + pltpu.roll(above, shift, 1)
                lower.append(
                    jnp.where(lane_slot == 0, below, pltpu.roll(pack_z[1, f, rows, :], EDGE, 1))
                )
                upper.append(
                    jnp.where(
                        lane_slot == owned - 1, above, pltpu.roll(pack_z[0, f, rows, :], LANES - EDGE, 1)
                    )
                )
            lower, _ = cell_fields(lower)
            upper, _ = cell_fields(upper)
            for f in range(FIELDS):
                for j in range(2):
                    tra[f, 2 * i + j + 4, 4:8, :] = lower[f][4 * j : 4 * j + 4]
                    tra[f, 2 * i + j + 4, 24:28, :] = upper[f][4 * j : 4 * j + 4]
        return carry

    lax.fori_loop(0, (EDGE // 2) // 4, third_halo, 0)

    def third_boundary(i, carry):
        for u in range(OUTER):
            y = OUTER * i + u
            total = line_boundary(tra, y + 4, 2)
            for f in range(5):
                for c in range(2):
                    rows = slice(8 * c, 8 * c + 8)
                    tend_t[f, y, rows, :] = tend_t[f, y, rows, :] + total[c][f]
        return carry

    lax.fori_loop(0, EDGE // OUTER, third_boundary, 0)
    copies[2].wait_recv()
    copies[3].wait_recv()

    def first_halo(group, carry):
        for i in [2 * group + u for u in range(2)]:
            rows = pl.ds(pl.multiple_of(8 * i, 8), 8)
            for side in range(2):
                at = 4 if side == 0 else 24
                for half in range(2):
                    lanes = slice(half * LANES, (half + 1) * LANES)
                    fields, _ = cell_fields([halo_x[side, f, rows, lanes] for f in range(5)])
                    for f in range(FIELDS):
                        for j in range(2):
                            nat[f, 2 * (2 * i + j) + half, at : at + 4, :] = fields[f][4 * j : 4 * j + 4]
        return carry

    lax.fori_loop(0, (CAP // 2) // 2, first_halo, 0)

    def first_boundary(i, carry):
        for u in range(OUTER):
            line = OUTER * i + u
            total = line_boundary(nat, line, 0)
            for f in range(5):
                for c in range(2):
                    rows = slice(8 * c, 8 * c + 8)
                    tend_x[f, line, rows, :] = tend_x[f, line, rows, :] + total[c][f]
        return carry

    lax.fori_loop(0, 2 * CAP // OUTER, first_boundary, 0)
    copies[4].wait_recv()
    copies[5].wait_recv()

    def second_halo(group, carry):
        for y in [2 * group + u for u in range(2)]:
            for side in range(2):
                for zt in range(2):
                    rows = slice(8 * zt, 8 * zt + 8)
                    fields, _ = cell_fields([halo_y[side, f, y, rows, :] for f in range(5)])
                    for f in range(FIELDS):
                        tra[f, y + 20 * side, 8 + 8 * zt : 16 + 8 * zt, :] = fields[f]
        return carry

    lax.fori_loop(0, (4) // 2, second_halo, 0)
    for y in range(4):
        for zt in range(2):
            rows = slice(8 * zt, 8 * zt + 8)
            low = [tend_t[f, y, rows, :] for f in range(5)]
            high = [tend_t[f, y + EDGE - 4, rows, :] for f in range(5)]
            for k in range(y + 1, 5):
                flux = plane_pair(y - k, k, zt)
                low = [low[f] - flux[f] for f in range(5)]
            for k in range(4 - y, 5):
                flux = plane_pair(y + EDGE - 4, k, zt)
                high = [high[f] + flux[f] for f in range(5)]
            for f in range(5):
                tend_t[f, y, rows, :] = low[f]
                tend_t[f, y + EDGE - 4, rows, :] = high[f]

    for f in range(5):
        for half in range(2):
            part = tend_t[f, half * 8 : (half + 1) * 8, :, :].reshape(LANES, LANES).T
            for s in range(CAP):
                value = part[s * EDGE : (s + 1) * EDGE] + tend_x[f, 2 * s + half, :, :]
                out_ref[s, f, :, half * LANES : (half + 1) * LANES] = (
                    2.0 * value if f == 4 else value
                )
    info_ref[1] = jnp.full((8, LANES), owned, jnp.int32).astype(jnp.float32)
    info_ref[0] = gather_peaks(2, owners + 2, y_copies)
    for copy in copies.values():
        copy.wait_send()
    reg_load.wait()


def update_kernel(tend_ref, info_ref, sol_ref, reg_ref, sol_hbm, reg_hbm, new_sol, new_reg, sems):
    fastest = jnp.max(info_ref[0], axis=(0, 1), keepdims=True)
    time_step = jnp.broadcast_to(COURANT / (EDGE * fastest), (EDGE, 2 * LANES))
    owned = jnp.broadcast_to(info_ref[1, 0:1, 0:1], (EDGE, 2 * LANES))
    copies = []
    for s in range(CAP):
        keep = owned > float(s)
        for f in range(5):
            register = LOW_STORAGE_A[SECTION] * reg_ref[s, f] + time_step * tend_ref[s, f]
            state = sol_ref[s, f] + LOW_STORAGE_B[SECTION] * register
            new_reg[s, f] = jnp.where(keep, register, 0.0)
            new_sol[s, f] = jnp.where(keep, state, 0.0)
        if s % 2 == 1:
            part = pl.ds(s - 1, 2)
            for i, (source, target) in enumerate(((new_reg, reg_hbm), (new_sol, sol_hbm))):
                copy = pltpu.make_async_copy(source.at[part], target.at[part], sems.at[i, s // 2])
                copy.start()
                copies.append(copy)
    for copy in copies:
        copy.wait()


def on_device(solution, register, counts):
    blocks, old_register = solution[0], register[0]
    shape = blocks.shape
    f32 = jnp.float32
    scratch = [
        pltpu.SMEM((OWNERS,), jnp.int32),
        pltpu.VMEM((5, EDGE, EDGE, LANES), f32),
        pltpu.VMEM((2, 5, 4 * CAP, 2 * LANES), f32),
        pltpu.VMEM((2, 5, 4 * EDGE, LANES), f32),
        pltpu.VMEM((2, 5, 4 * CAP, 2 * LANES), f32),
        pltpu.VMEM((2, 5, 4, EDGE, LANES), f32),
        pltpu.VMEM((2, 5, 4 * EDGE, LANES), f32),
        pltpu.VMEM((FIELDS, 2 * CAP, 32, LANES), f32),
        pltpu.VMEM((FIELDS, EDGE + 8, 32, LANES), f32),
        pltpu.VMEM((2, 4, 5, 24, LANES), f32),
        pltpu.VMEM((4, 5, EDGE + 4, EDGE, LANES), f32),
        pltpu.VMEM((5, 2 * CAP, EDGE, LANES), f32),
        pltpu.VMEM((5, EDGE, EDGE, LANES), f32),
        pltpu.VMEM((3, 8, LANES), f32),
        pltpu.VMEM((13, 8, LANES), f32),
        pltpu.SemaphoreType.DMA((CAP,)),
        pltpu.SemaphoreType.DMA,
        pltpu.SemaphoreType.DMA,
        pltpu.SemaphoreType.DMA((6,)),
        pltpu.SemaphoreType.DMA((6,)),
        pltpu.SemaphoreType.DMA((13,)),
        pltpu.SemaphoreType.DMA((13,)),
    ]
    cells = jax.ShapeDtypeStruct(shape, f32)
    tendency, info, state, past = pl.pallas_call(
        tendency_kernel,
        out_shape=[cells, jax.ShapeDtypeStruct((2, 8, LANES), f32), cells, cells],
        in_specs=[pl.BlockSpec(memory_space=pltpu.HBM)] * 3,
        out_specs=[pl.BlockSpec(memory_space=pltpu.VMEM)] * 4,
        scratch_shapes=scratch,
        compiler_params=pltpu.CompilerParams(
            collective_id=0, has_side_effects=True, vmem_limit_bytes=20 * 2**20
        ),
        name="tendency",
    )(
        pltpu.with_memory_space_constraint(counts, pltpu.HBM),
        pltpu.with_memory_space_constraint(blocks, pltpu.HBM),
        pltpu.with_memory_space_constraint(old_register, pltpu.HBM),
    )
    new_solution, new_register = pl.pallas_call(
        update_kernel,
        out_shape=[jax.ShapeDtypeStruct(shape, f32)] * 2,
        in_specs=[pl.BlockSpec(memory_space=pltpu.VMEM)] * 4,
        out_specs=[pl.BlockSpec(memory_space=pltpu.HBM)] * 2,
        scratch_shapes=[
            pltpu.VMEM(shape, f32),
            pltpu.VMEM(shape, f32),
            pltpu.SemaphoreType.DMA((2, CAP // 2)),
        ],
        compiler_params=pltpu.CompilerParams(vmem_limit_bytes=8 * 2**20),
        name="update",
    )(tendency, info, state, past)
    return (new_solution[None], new_register[None])


def solution(mesh):
    in_specs = (P("group", "block", None, None, None), P("group", "block", None, None, None), P())
    out_specs = (P("group", "block", None, None, None), P("group", "block", None, None, None))
    return jax.shard_map(
        on_device, mesh=mesh, in_specs=in_specs, out_specs=out_specs, check_vma=False
    )
```

```python
import functools

import jax
import jax.numpy as jnp
from jax import lax
from jax.experimental import pallas as pl
from jax.experimental.pallas import tpu as pltpu
from jax.sharding import PartitionSpec as P

SECTION = 2
HEAT_RATIO = 1.4
COURANT = 0.5
SERIES_CUT = 0.0001
CENTRAL_WEIGHTS = (0.8, -0.2, 4.0 / 105.0, -1.0 / 280.0)
LOW_STORAGE_A = (
    0.0,
    -567301805773.0 / 1357537059087.0,
    -2404267990393.0 / 2016746695238.0,
    -3550918686646.0 / 2091501179385.0,
    -1275806237668.0 / 842570457699.0,
)
LOW_STORAGE_B = (
    1432997174477.0 / 9575080441755.0,
    5161836677717.0 / 13612068292357.0,
    1720146321549.0 / 2090206949498.0,
    3134564353537.0 / 4481467310338.0,
    2277821191437.0 / 14882151754819.0,
)
MESH = pl.DeviceIdType.MESH
EDGE = 16
CAP = 8
OWNERS = 8
LANES = 128
FIELDS = 8
INNER = 2
OUTER = 2


def cell_fields(state):
    density, first, second, third, energy = state
    inverse = 1.0 / density
    v1, v2, v3 = first * inverse, second * inverse, third * inverse
    pressure = (HEAT_RATIO - 1.0) * (energy - 0.5 * (first * v1 + second * v2 + third * v3))
    half_log = 0.5 * jnp.log(density)
    half_log_p = 0.5 * jnp.log(pressure)
    fields = [
        0.5 * density,
        0.5 * v1,
        0.5 * v2,
        0.5 * v3,
        0.5 * pressure,
        half_log,
        (HEAT_RATIO - 1.0) * (density / pressure),
        half_log - half_log_p,
    ]
    return fields, (v1, v2, v3, pressure, inverse)


def mean_parts(left, right, left_log, right_log):
    total = left + right
    step = right - left
    ratio = step / total
    ratio_sq = ratio * ratio
    near = ratio_sq < SERIES_CUT
    series = 1.0 + ratio_sq * (1.0 / 3.0 + ratio_sq * (1.0 / 5.0 + ratio_sq * (1.0 / 7.0)))
    return jnp.where(near, total, step), jnp.where(near, series, right_log - left_log)


def pair_flux(left, right, direction, factor):
    means = [left[1 + m] + right[1 + m] for m in range(3)]
    products = left[1] * right[1] + left[2] * right[2] + left[3] * right[3]
    top, bottom = mean_parts(left[0], right[0], left[5], right[5])
    top_t, bottom_t = mean_parts(left[6], right[6], left[7], right[7])
    mass = (top / bottom) * (factor * means[direction])
    inverse_mean = bottom_t / top_t
    momenta = [mass * means[m] for m in range(3)]
    momenta[direction] = momenta[direction] + factor * (left[4] + right[4])
    cross = left[4] * right[1 + direction] + right[4] * left[1 + direction]
    energy = mass * (products + inverse_mean) + factor * cross
    return [mass] + momenta + [energy]


FACTORS = tuple(-float(EDGE) * 2.0 * weight for weight in CENTRAL_WEIGHTS)


def tendency_kernel(
    counts_hbm,
    sol_hbm,
    reg_hbm,
    out_ref,
    info_ref,
    sol,
    reg,
    counts_ref,
    cons,
    pack_x,
    pack_z,
    halo_x,
    halo_y,
    halo_z,
    nat,
    tra,
    line_flux,
    plane_flux,
    tend_x,
    tend_t,
    edge_t,
    peak,
    peak_in,
    load_sem,
    counts_sem,
    reg_sem,
    send_sem,
    recv_sem,
    peak_send,
    peak_recv,
):
    g = lax.axis_index("group")
    b = lax.axis_index("block")
    groups = lax.axis_size("group")
    owners = lax.axis_size("block")
    shear = groups // 4
    zdim = groups // shear
    base = (g // zdim) * zdim
    block_peers = [(g, lax.rem(b + j, owners)) for j in range(1, owners)]
    y_peers = [(lax.rem(g + shear * j, groups), b) for j in range(1, 4)]
    z_peers = [(base + lax.rem(g - base + j, zdim), b) for j in range(1, zdim)]
    up_y, down_y = (lax.rem(g + 1, groups), b), (lax.rem(g + groups - 1, groups), b)
    up_x, down_x = y_peers[0], y_peers[2]
    up_z, down_z = block_peers[0], block_peers[-1]

    counts_load = pltpu.make_async_copy(counts_hbm, counts_ref, counts_sem)
    counts_load.start()
    loads = [pltpu.make_async_copy(sol_hbm.at[s], sol.at[s], load_sem.at[s]) for s in range(CAP)]
    for load in loads:
        load.start()
    barrier = pltpu.get_barrier_semaphore()
    everyone = [up_y, down_y] + y_peers + z_peers + block_peers
    for peer in everyone:
        pl.semaphore_signal(barrier, inc=1, device_id=peer, device_id_type=MESH)
    reg_load = pltpu.make_async_copy(reg_hbm, reg, reg_sem)
    reg_load.start()
    counts_load.wait()
    owned = counts_ref[b]
    owned_below = counts_ref[lax.rem(b + owners - 1, owners)]
    lane_slot = lax.broadcasted_iota(jnp.int32, (8, LANES), 1) // EDGE

    def natural_fields(s, fastest):
        pltpu.make_async_copy(sol_hbm.at[s], sol.at[s], load_sem.at[s]).wait()
        used = jnp.full((8, LANES), s, jnp.int32) < owned
        for half in range(2):
            for rt in range(2):
                fields, (v1, v2, v3, pressure, inverse) = cell_fields(
                    [
                        sol[s, f, 8 * rt : 8 * rt + 8, half * LANES : (half + 1) * LANES]
                        for f in range(5)
                    ]
                )
                for f in range(FIELDS):
                    nat[f, 2 * s + half, 8 + 8 * rt : 16 + 8 * rt, :] = fields[f]
                    if rt == 1:
                        nat[f, 2 * s + half, 24:32, :] = fields[f]
                speed = jnp.sqrt(v1 * v1 + v2 * v2 + v3 * v3) + jnp.sqrt(
                    HEAT_RATIO * pressure * inverse
                )
                fastest = jnp.maximum(fastest, jnp.where(used, speed, 0.0))
        return fastest

    peak[0] = lax.fori_loop(0, CAP, natural_fields, jnp.zeros((8, LANES), jnp.float32))

    for f in range(5):
        for s in range(CAP):
            pack_x[0, f, 4 * s : 4 * s + 4, :] = sol[s, f, 0:4, :]
            pack_x[1, f, 4 * s : 4 * s + 4, :] = sol[s, f, EDGE - 4 : EDGE, :]
    for f in range(5):
        for half in range(2):
            part = sol[:, f, :, half * LANES : (half + 1) * LANES].reshape(LANES, LANES)
            cons[f, half * 8 : (half + 1) * 8, :, :] = part.T.reshape(8, EDGE, LANES)
    for f in range(5):
        for y in range(EDGE):
            pack_z[0, f, 4 * y : 4 * y + 4, :] = cons[f, y, 0:4, :]
            pack_z[1, f, 4 * y : 4 * y + 4, :] = cons[f, y, EDGE - 4 : EDGE, :]

    def exchange_peaks(stage, first, peers):
        started = []
        for j, peer in enumerate(peers):
            copy = pltpu.make_async_remote_copy(
                src_ref=peak.at[stage],
                dst_ref=peak_in.at[first + j],
                send_sem=peak_send.at[first + j],
                recv_sem=peak_recv.at[first + j],
                device_id=peer,
                device_id_type=MESH,
            )
            copy.start()
            started.append(copy)
        return started

    def gather_peaks(stage, first, started):
        value = peak[stage]
        for j, copy in enumerate(started):
            copy.wait()
            value = jnp.maximum(value, peak_in[first + j])
        return value

    def send(index, source, target, peer):
        copy = pltpu.make_async_remote_copy(
            src_ref=source,
            dst_ref=target,
            send_sem=send_sem.at[index],
            recv_sem=recv_sem.at[index],
            device_id=peer,
            device_id_type=MESH,
        )
        copy.start()
        return copy

    pl.semaphore_wait(barrier, len(everyone))
    copies = {
        4: send(4, cons.at[:, EDGE - 4 : EDGE], halo_y.at[0], up_y),
        5: send(5, cons.at[:, 0:4], halo_y.at[1], down_y),
    }
    block_copies = exchange_peaks(0, 0, block_peers)
    copies[2] = send(2, pack_x.at[1], halo_x.at[0], up_x)
    copies[3] = send(3, pack_x.at[0], halo_x.at[1], down_x)
    copies[0] = send(0, pack_z.at[1], halo_z.at[0], up_z)
    copies[1] = send(1, pack_z.at[0], halo_z.at[1], down_z)

    def transposed_fields(group, carry):
        for y in [2 * group + u for u in range(2)]:
            for zt in range(2):
                rows = slice(8 * zt, 8 * zt + 8)
                fields = cell_fields([cons[f, y, rows, :] for f in range(5)])[0]
                for f in range(FIELDS):
                    tra[f, y + 4, 8 + 8 * zt : 16 + 8 * zt, :] = fields[f]
                    if zt == 1:
                        tra[f, y + 4, 24:32, :] = fields[f]
        return carry

    lax.fori_loop(0, (EDGE) // 2, transposed_fields, 0)


    row = lax.broadcasted_iota(jnp.int32, (8, LANES), 0)
    is_low = row < 4
    inner = [jnp.where(row < 8 - k, FACTORS[k - 1], 0.0) for k in range(1, 5)]
    outer = [
        jnp.where(
            is_low,
            jnp.where(row < k, -FACTORS[k - 1], 0.0),
            jnp.where(row >= 8 - k, FACTORS[k - 1], 0.0),
        )
        for k in range(1, 5)
    ]
    for u in range(2):
        for k in range(4):
            for f in range(5):
                line_flux[u, k, f, 0:8, :] = jnp.zeros((8, LANES), jnp.float32)

    def line_interior(ref, line, direction, u):
        left = [
            [ref[f, line, 8 + 8 * c : 16 + 8 * c, :] for f in range(FIELDS)] for c in range(2)
        ]
        total = [[None] * 5 for c in range(2)]
        for k in range(1, 5):
            for c in range(2):
                at = 8 + 8 * c
                flux = pair_flux(
                    left[c],
                    [ref[f, line, at + k : at + 8 + k, :] for f in range(FIELDS)],
                    direction,
                    inner[k - 1] if c == 1 else FACTORS[k - 1],
                )
                for f in range(5):
                    line_flux[u, k - 1, f, at : at + 8, :] = flux[f]
                    total[c][f] = flux[f] if k == 1 else total[c][f] + flux[f]
            for c in range(2):
                at = 8 + 8 * c
                for f in range(5):
                    total[c][f] = total[c][f] - line_flux[u, k - 1, f, at - k : at + 8 - k, :]
        return total

    def line_boundary(ref, line, direction):
        first_rows = [ref[f, line, 8:16, :] for f in range(FIELDS)]
        last_rows = [ref[f, line, 16:24, :] for f in range(FIELDS)]
        total = [None] * 5
        for k in range(1, 5):
            flux = pair_flux(
                [
                    jnp.where(is_low, ref[f, line, 8 - k : 16 - k, :], last_rows[f])
                    for f in range(FIELDS)
                ],
                [
                    jnp.where(is_low, first_rows[f], ref[f, line, 16 + k : 24 + k, :])
                    for f in range(FIELDS)
                ],
                direction,
                outer[k - 1],
            )
            for f in range(5):
                total[f] = flux[f] if k == 1 else total[f] + flux[f]
        return [jnp.where(is_low, t, 0.0) for t in total], [jnp.where(is_low, 0.0, t) for t in total]

    def plane_pair(y, k, zt):
        rows = slice(8 + 8 * zt, 16 + 8 * zt)
        return pair_flux(
            [tra[f, y + 4, rows, :] for f in range(FIELDS)],
            [tra[f, y + 4 + k, rows, :] for f in range(FIELDS)],
            1,
            FACTORS[k - 1],
        )

    def ahead(y, offsets):
        for zt in range(2):
            rows = slice(8 * zt, 8 * zt + 8)
            total = [None] * 5
            for k in offsets:
                flux = plane_pair(y, k, zt)
                for f in range(5):
                    plane_flux[k - 1, f, y + 4, rows, :] = flux[f]
                    total[f] = flux[f] if total[f] is None else total[f] + flux[f]
            for f in range(5):
                tend_t[f, y, rows, :] = total[f]

    def second_interior(y, carry):
        ahead(y, range(1, 5))
        return carry

    lax.fori_loop(0, EDGE - 4, second_interior, 0)
    for y in range(EDGE - 4, EDGE - 1):
        ahead(y, range(1, EDGE - y))
    for f in range(5):
        tend_t[f, EDGE - 1, :, :] = jnp.zeros((EDGE, LANES), jnp.float32)

    peak[1] = gather_peaks(0, 0, block_copies)
    z_copies = exchange_peaks(1, owners - 1, z_peers)

    def behind(y, offsets):
        for zt in range(2):
            rows = slice(8 * zt, 8 * zt + 8)
            for f in range(5):
                total = tend_t[f, y, rows, :]
                for k in offsets:
                    total = total - plane_flux[k - 1, f, y + 4 - k, rows, :]
                tend_t[f, y, rows, :] = total

    def second_behind(y, carry):
        behind(y, range(1, 5))
        return carry

    for y in range(1, 4):
        behind(y, range(1, y + 1))
    lax.fori_loop(4, EDGE, second_behind, 0)

    def third_line(i, carry):
        for u in range(INNER):
            y = INNER * i + u
            total = line_interior(tra, y + 4, 2, u)
            for f in range(5):
                for c in range(2):
                    rows = slice(8 * c, 8 * c + 8)
                    tend_t[f, y, rows, :] = tend_t[f, y, rows, :] + total[c][f]
        return carry

    def first_line(i, carry):
        for u in range(INNER):
            line = INNER * i + u
            total = line_interior(nat, line, 0, u)
            for f in range(5):
                for c in range(2):
                    tend_x[f, line, 8 * c : 8 * c + 8, :] = total[c][f]
        return carry

    lax.fori_loop(0, EDGE // INNER, third_line, 0)
    lax.fori_loop(0, CAP // INNER, first_line, 0)
    peak[2] = gather_peaks(1, owners - 1, z_copies)
    y_copies = exchange_peaks(2, owners + 2, y_peers)
    lax.fori_loop(CAP // INNER, 2 * CAP // INNER, first_line, 0)

    copies[0].wait_recv()
    copies[1].wait_recv()

    def third_halo(group, carry):
        for i in [4 * group + u for u in range(4)]:
            rows = pl.ds(pl.multiple_of(8 * i, 8), 8)
            lower, upper = [], []
            for f in range(5):
                below = jnp.where(lane_slot == owned_below - 1, halo_z[0, f, rows, :], 0.0)
                above = jnp.where(lane_slot == 0, halo_z[1, f, rows, :], 0.0)
                for shift in (16, 32, 64):
                    below = below + pltpu.roll(below, shift, 1)
                    above = above + pltpu.roll(above, shift, 1)
                lower.append(
                    jnp.where(lane_slot == 0, below, pltpu.roll(pack_z[1, f, rows, :], EDGE, 1))
                )
                upper.append(
                    jnp.where(
                        lane_slot == owned - 1, above, pltpu.roll(pack_z[0, f, rows, :], LANES - EDGE, 1)
                    )
                )
            lower, _ = cell_fields(lower)
            upper, _ = cell_fields(upper)
            for f in range(FIELDS):
                for j in range(2):
                    tra[f, 2 * i + j + 4, 4:8, :] = lower[f][4 * j : 4 * j + 4]
                    tra[f, 2 * i + j + 4, 24:28, :] = upper[f][4 * j : 4 * j + 4]
        return carry

    lax.fori_loop(0, (EDGE // 2) // 4, third_halo, 0)

    def third_boundary(i, carry):
        for u in range(OUTER):
            y = OUTER * i + u
            total = line_boundary(tra, y + 4, 2)
            for f in range(5):
                for c in range(2):
                    rows = slice(8 * c, 8 * c + 8)
                    tend_t[f, y, rows, :] = tend_t[f, y, rows, :] + total[c][f]
        return carry

    lax.fori_loop(0, EDGE // OUTER, third_boundary, 0)
    copies[2].wait_recv()
    copies[3].wait_recv()

    def first_halo(group, carry):
        for i in [2 * group + u for u in range(2)]:
            rows = pl.ds(pl.multiple_of(8 * i, 8), 8)
            for side in range(2):
                at = 4 if side == 0 else 24
                for half in range(2):
                    lanes = slice(half * LANES, (half + 1) * LANES)
                    fields, _ = cell_fields([halo_x[side, f, rows, lanes] for f in range(5)])
                    for f in range(FIELDS):
                        for j in range(2):
                            nat[f, 2 * (2 * i + j) + half, at : at + 4, :] = fields[f][4 * j : 4 * j + 4]
        return carry

    lax.fori_loop(0, (CAP // 2) // 2, first_halo, 0)

    def first_boundary(i, carry):
        for u in range(OUTER):
            line = OUTER * i + u
            total = line_boundary(nat, line, 0)
            for f in range(5):
                for c in range(2):
                    rows = slice(8 * c, 8 * c + 8)
                    tend_x[f, line, rows, :] = tend_x[f, line, rows, :] + total[c][f]
        return carry

    lax.fori_loop(0, 2 * CAP // OUTER, first_boundary, 0)
    for f in range(5):
        for half in range(2):
            part = tend_t[f, half * 8 : (half + 1) * 8, :, :].reshape(LANES, LANES).T
            for s in range(CAP):
                value = part[s * EDGE : (s + 1) * EDGE] + tend_x[f, 2 * s + half, :, :]
                out_ref[s, f, :, half * LANES : (half + 1) * LANES] = (
                    2.0 * value if f == 4 else value
                )
    copies[4].wait_recv()
    copies[5].wait_recv()

    def second_halo(group, carry):
        for y in [2 * group + u for u in range(2)]:
            for side in range(2):
                for zt in range(2):
                    rows = slice(8 * zt, 8 * zt + 8)
                    fields, _ = cell_fields([halo_y[side, f, y, rows, :] for f in range(5)])
                    for f in range(FIELDS):
                        tra[f, y + 20 * side, 8 + 8 * zt : 16 + 8 * zt, :] = fields[f]
        return carry

    lax.fori_loop(0, (4) // 2, second_halo, 0)
    for y in range(4):
        for zt in range(2):
            rows = slice(8 * zt, 8 * zt + 8)
            low, high = [None] * 5, [None] * 5
            for k in range(y + 1, 5):
                flux = plane_pair(y - k, k, zt)
                low = [-flux[f] if low[f] is None else low[f] - flux[f] for f in range(5)]
            for k in range(4 - y, 5):
                flux = plane_pair(y + EDGE - 4, k, zt)
                high = [flux[f] if high[f] is None else high[f] + flux[f] for f in range(5)]
            for f in range(5):
                edge_t[f, y, rows, :] = low[f]
                edge_t[f, y + 4, rows, :] = high[f]

    left_lanes = lax.broadcasted_iota(jnp.int32, (EDGE, LANES), 1) < LANES // 2
    for f in range(5):
        part = edge_t[f].reshape(LANES, LANES).T
        for s in range(CAP):
            value = part[s * EDGE : (s + 1) * EDGE]
            if f == 4:
                value = 2.0 * value
            for half in range(2):
                lanes = slice(half * LANES, (half + 1) * LANES)
                mine = left_lanes if half == 0 else jnp.logical_not(left_lanes)
                out_ref[s, f, :, lanes] = out_ref[s, f, :, lanes] + jnp.where(mine, value, 0.0)
    info_ref[1] = jnp.full((8, LANES), owned, jnp.int32).astype(jnp.float32)
    info_ref[0] = gather_peaks(2, owners + 2, y_copies)
    for copy in copies.values():
        copy.wait_send()
    reg_load.wait()


def update_kernel(tend_ref, info_ref, sol_ref, reg_ref, sol_hbm, reg_hbm, new_sol, new_reg, sems):
    fastest = jnp.max(info_ref[0], axis=(0, 1), keepdims=True)
    time_step = jnp.broadcast_to(COURANT / (EDGE * fastest), (EDGE, 2 * LANES))
    owned = jnp.broadcast_to(info_ref[1, 0:1, 0:1], (EDGE, 2 * LANES))
    copies = []
    for s in range(CAP):
        keep = owned > float(s)
        for f in range(5):
            register = LOW_STORAGE_A[SECTION] * reg_ref[s, f] + time_step * tend_ref[s, f]
            state = sol_ref[s, f] + LOW_STORAGE_B[SECTION] * register
            new_reg[s, f] = jnp.where(keep, register, 0.0)
            new_sol[s, f] = jnp.where(keep, state, 0.0)
        if s % 2 == 1:
            part = pl.ds(s - 1, 2)
            for i, (source, target) in enumerate(((new_reg, reg_hbm), (new_sol, sol_hbm))):
                copy = pltpu.make_async_copy(source.at[part], target.at[part], sems.at[i, s // 2])
                copy.start()
                copies.append(copy)
    for copy in copies:
        copy.wait()


def on_device(solution, register, counts):
    blocks, old_register = solution[0], register[0]
    shape = blocks.shape
    f32 = jnp.float32
    scratch = [
        pltpu.SMEM((OWNERS,), jnp.int32),
        pltpu.VMEM((5, EDGE, EDGE, LANES), f32),
        pltpu.VMEM((2, 5, 4 * CAP, 2 * LANES), f32),
        pltpu.VMEM((2, 5, 4 * EDGE, LANES), f32),
        pltpu.VMEM((2, 5, 4 * CAP, 2 * LANES), f32),
        pltpu.VMEM((2, 5, 4, EDGE, LANES), f32),
        pltpu.VMEM((2, 5, 4 * EDGE, LANES), f32),
        pltpu.VMEM((FIELDS, 2 * CAP, 32, LANES), f32),
        pltpu.VMEM((FIELDS, EDGE + 8, 32, LANES), f32),
        pltpu.VMEM((2, 4, 5, 24, LANES), f32),
        pltpu.VMEM((4, 5, EDGE + 4, EDGE, LANES), f32),
        pltpu.VMEM((5, 2 * CAP, EDGE, LANES), f32),
        pltpu.VMEM((5, EDGE, EDGE, LANES), f32),
        pltpu.VMEM((5, 8, EDGE, LANES), f32),
        pltpu.VMEM((3, 8, LANES), f32),
        pltpu.VMEM((13, 8, LANES), f32),
        pltpu.SemaphoreType.DMA((CAP,)),
        pltpu.SemaphoreType.DMA,
        pltpu.SemaphoreType.DMA,
        pltpu.SemaphoreType.DMA((6,)),
        pltpu.SemaphoreType.DMA((6,)),
        pltpu.SemaphoreType.DMA((13,)),
        pltpu.SemaphoreType.DMA((13,)),
    ]
    cells = jax.ShapeDtypeStruct(shape, f32)
    tendency, info, state, past = pl.pallas_call(
        tendency_kernel,
        out_shape=[cells, jax.ShapeDtypeStruct((2, 8, LANES), f32), cells, cells],
        in_specs=[pl.BlockSpec(memory_space=pltpu.HBM)] * 3,
        out_specs=[pl.BlockSpec(memory_space=pltpu.VMEM)] * 4,
        scratch_shapes=scratch,
        compiler_params=pltpu.CompilerParams(
            collective_id=0, has_side_effects=True, vmem_limit_bytes=20 * 2**20
        ),
        name="tendency",
    )(
        pltpu.with_memory_space_constraint(counts, pltpu.HBM),
        pltpu.with_memory_space_constraint(blocks, pltpu.HBM),
        pltpu.with_memory_space_constraint(old_register, pltpu.HBM),
    )
    new_solution, new_register = pl.pallas_call(
        update_kernel,
        out_shape=[jax.ShapeDtypeStruct(shape, f32)] * 2,
        in_specs=[pl.BlockSpec(memory_space=pltpu.VMEM)] * 4,
        out_specs=[pl.BlockSpec(memory_space=pltpu.HBM)] * 2,
        scratch_shapes=[
            pltpu.VMEM(shape, f32),
            pltpu.VMEM(shape, f32),
            pltpu.SemaphoreType.DMA((2, CAP // 2)),
        ],
        compiler_params=pltpu.CompilerParams(vmem_limit_bytes=8 * 2**20),
        name="update",
    )(tendency, info, state, past)
    return (new_solution[None], new_register[None])


def solution(mesh):
    in_specs = (P("group", "block", None, None, None), P("group", "block", None, None, None), P())
    out_specs = (P("group", "block", None, None, None), P("group", "block", None, None, None))
    return jax.shard_map(
        on_device, mesh=mesh, in_specs=in_specs, out_specs=out_specs, check_vma=False
    )
```

```python
import functools

import jax
import jax.numpy as jnp
from jax import lax
from jax.experimental import pallas as pl
from jax.experimental.pallas import tpu as pltpu
from jax.sharding import PartitionSpec as P

SECTION = 2
HEAT_RATIO = 1.4
COURANT = 0.5
SERIES_CUT = 0.0001
CENTRAL_WEIGHTS = (0.8, -0.2, 4.0 / 105.0, -1.0 / 280.0)
LOW_STORAGE_A = (
    0.0,
    -567301805773.0 / 1357537059087.0,
    -2404267990393.0 / 2016746695238.0,
    -3550918686646.0 / 2091501179385.0,
    -1275806237668.0 / 842570457699.0,
)
LOW_STORAGE_B = (
    1432997174477.0 / 9575080441755.0,
    5161836677717.0 / 13612068292357.0,
    1720146321549.0 / 2090206949498.0,
    3134564353537.0 / 4481467310338.0,
    2277821191437.0 / 14882151754819.0,
)
MESH = pl.DeviceIdType.MESH
EDGE = 16
CAP = 8
OWNERS = 8
LANES = 128
FIELDS = 8
INNER = 2
OUTER = 2


def cell_fields(state):
    density, first, second, third, energy = state
    inverse = 1.0 / density
    v1, v2, v3 = first * inverse, second * inverse, third * inverse
    pressure = (HEAT_RATIO - 1.0) * (energy - 0.5 * (first * v1 + second * v2 + third * v3))
    half_log = 0.5 * jnp.log(density)
    half_log_p = 0.5 * jnp.log(pressure)
    fields = [
        0.5 * density,
        0.5 * v1,
        0.5 * v2,
        0.5 * v3,
        0.5 * pressure,
        half_log,
        (HEAT_RATIO - 1.0) * (density / pressure),
        half_log - half_log_p,
    ]
    return fields, (v1, v2, v3, pressure, inverse)


def mean_parts(left, right, left_log, right_log):
    total = left + right
    step = right - left
    ratio = step / total
    ratio_sq = ratio * ratio
    near = ratio_sq < SERIES_CUT
    series = 1.0 + ratio_sq * (1.0 / 3.0 + ratio_sq * (1.0 / 5.0 + ratio_sq * (1.0 / 7.0)))
    return jnp.where(near, total, step), jnp.where(near, series, right_log - left_log)


def pair_flux(left, right, direction, factor):
    means = [left[1 + m] + right[1 + m] for m in range(3)]
    products = left[1] * right[1] + left[2] * right[2] + left[3] * right[3]
    top, bottom = mean_parts(left[0], right[0], left[5], right[5])
    top_t, bottom_t = mean_parts(left[6], right[6], left[7], right[7])
    mass = (top / bottom) * (factor * means[direction])
    inverse_mean = bottom_t / top_t
    momenta = [mass * means[m] for m in range(3)]
    momenta[direction] = momenta[direction] + factor * (left[4] + right[4])
    cross = left[4] * right[1 + direction] + right[4] * left[1 + direction]
    energy = mass * (products + inverse_mean) + factor * cross
    return [mass] + momenta + [energy]


FACTORS = tuple(-float(EDGE) * 2.0 * weight for weight in CENTRAL_WEIGHTS)


def tendency_kernel(
    counts_hbm,
    sol_hbm,
    reg_hbm,
    out_ref,
    info_ref,
    sol,
    reg,
    counts_ref,
    cons,
    pack_x,
    pack_z,
    halo_x,
    halo_y,
    halo_z,
    nat,
    tra,
    line_flux,
    plane_flux,
    tend_x,
    tend_t,
    edge_t,
    peak,
    peak_in,
    load_sem,
    counts_sem,
    reg_sem,
    send_sem,
    recv_sem,
    peak_send,
    peak_recv,
):
    g = lax.axis_index("group")
    b = lax.axis_index("block")
    groups = lax.axis_size("group")
    owners = lax.axis_size("block")
    shear = groups // 4
    zdim = groups // shear
    base = (g // zdim) * zdim
    block_peers = [(g, lax.rem(b + j, owners)) for j in range(1, owners)]
    y_peers = [(lax.rem(g + shear * j, groups), b) for j in range(1, 4)]
    z_peers = [(base + lax.rem(g - base + j, zdim), b) for j in range(1, zdim)]
    up_y, down_y = (lax.rem(g + 1, groups), b), (lax.rem(g + groups - 1, groups), b)
    up_x, down_x = y_peers[0], y_peers[2]
    up_z, down_z = block_peers[0], block_peers[-1]

    counts_load = pltpu.make_async_copy(counts_hbm, counts_ref, counts_sem)
    counts_load.start()
    loads = [pltpu.make_async_copy(sol_hbm.at[s], sol.at[s], load_sem.at[s]) for s in range(CAP)]
    for load in loads:
        load.start()
    barrier = pltpu.get_barrier_semaphore()
    everyone = [up_y, down_y] + y_peers + z_peers + block_peers
    for peer in everyone:
        pl.semaphore_signal(barrier, inc=1, device_id=peer, device_id_type=MESH)
    reg_load = pltpu.make_async_copy(reg_hbm, reg, reg_sem)
    reg_load.start()
    counts_load.wait()
    owned = counts_ref[b]
    owned_below = counts_ref[lax.rem(b + owners - 1, owners)]
    lane_slot = lax.broadcasted_iota(jnp.int32, (8, LANES), 1) // EDGE

    def natural_fields(s, fastest):
        pltpu.make_async_copy(sol_hbm.at[s], sol.at[s], load_sem.at[s]).wait()
        used = jnp.full((8, LANES), s, jnp.int32) < owned
        for half in range(2):
            for rt in range(2):
                fields, (v1, v2, v3, pressure, inverse) = cell_fields(
                    [
                        sol[s, f, 8 * rt : 8 * rt + 8, half * LANES : (half + 1) * LANES]
                        for f in range(5)
                    ]
                )
                for f in range(FIELDS):
                    nat[f, 2 * s + half, 8 + 8 * rt : 16 + 8 * rt, :] = fields[f]
                    if rt == 1:
                        nat[f, 2 * s + half, 24:32, :] = fields[f]
                speed = jnp.sqrt(v1 * v1 + v2 * v2 + v3 * v3) + jnp.sqrt(
                    HEAT_RATIO * pressure * inverse
                )
                fastest = jnp.maximum(fastest, jnp.where(used, speed, 0.0))
        return fastest

    peak[0] = lax.fori_loop(0, CAP, natural_fields, jnp.zeros((8, LANES), jnp.float32))

    for f in range(5):
        for s in range(CAP):
            pack_x[0, f, 4 * s : 4 * s + 4, :] = sol[s, f, 0:4, :]
            pack_x[1, f, 4 * s : 4 * s + 4, :] = sol[s, f, EDGE - 4 : EDGE, :]
    def exchange_peaks(stage, first, peers):
        started = []
        for j, peer in enumerate(peers):
            copy = pltpu.make_async_remote_copy(
                src_ref=peak.at[stage],
                dst_ref=peak_in.at[first + j],
                send_sem=peak_send.at[first + j],
                recv_sem=peak_recv.at[first + j],
                device_id=peer,
                device_id_type=MESH,
            )
            copy.start()
            started.append(copy)
        return started

    def gather_peaks(stage, first, started):
        value = peak[stage]
        for j, copy in enumerate(started):
            copy.wait()
            value = jnp.maximum(value, peak_in[first + j])
        return value

    def send(index, source, target, peer):
        copy = pltpu.make_async_remote_copy(
            src_ref=source,
            dst_ref=target,
            send_sem=send_sem.at[index],
            recv_sem=recv_sem.at[index],
            device_id=peer,
            device_id_type=MESH,
        )
        copy.start()
        return copy

    pl.semaphore_wait(barrier, len(everyone))
    block_copies = exchange_peaks(0, 0, block_peers)
    for f in range(5):
        for half in range(2):
            part = sol[:, f, :, half * LANES : (half + 1) * LANES].reshape(LANES, LANES)
            cons[f, half * 8 : (half + 1) * 8, :, :] = part.T.reshape(8, EDGE, LANES)
    for f in range(5):
        for y in range(EDGE):
            pack_z[0, f, 4 * y : 4 * y + 4, :] = cons[f, y, 0:4, :]
            pack_z[1, f, 4 * y : 4 * y + 4, :] = cons[f, y, EDGE - 4 : EDGE, :]

    copies = {
        4: send(4, cons.at[:, EDGE - 4 : EDGE], halo_y.at[0], up_y),
        5: send(5, cons.at[:, 0:4], halo_y.at[1], down_y),
    }
    copies[2] = send(2, pack_x.at[1], halo_x.at[0], up_x)
    copies[3] = send(3, pack_x.at[0], halo_x.at[1], down_x)
    copies[0] = send(0, pack_z.at[1], halo_z.at[0], up_z)
    copies[1] = send(1, pack_z.at[0], halo_z.at[1], down_z)

    def transposed_fields(group, carry):
        for y in [2 * group + u for u in range(2)]:
            for zt in range(2):
                rows = slice(8 * zt, 8 * zt + 8)
                fields = cell_fields([cons[f, y, rows, :] for f in range(5)])[0]
                for f in range(FIELDS):
                    tra[f, y + 4, 8 + 8 * zt : 16 + 8 * zt, :] = fields[f]
                    if zt == 1:
                        tra[f, y + 4, 24:32, :] = fields[f]
        return carry

    lax.fori_loop(0, (EDGE) // 2, transposed_fields, 0)


    row = lax.broadcasted_iota(jnp.int32, (8, LANES), 0)
    is_low = row < 4
    inner = [jnp.where(row < 8 - k, FACTORS[k - 1], 0.0) for k in range(1, 5)]
    outer = [
        jnp.where(
            is_low,
            jnp.where(row < k, -FACTORS[k - 1], 0.0),
            jnp.where(row >= 8 - k, FACTORS[k - 1], 0.0),
        )
        for k in range(1, 5)
    ]
    for u in range(2):
        for k in range(4):
            for f in range(5):
                line_flux[u, k, f, 0:8, :] = jnp.zeros((8, LANES), jnp.float32)

    def line_interior(ref, line, direction, u):
        left = [
            [ref[f, line, 8 + 8 * c : 16 + 8 * c, :] for f in range(FIELDS)] for c in range(2)
        ]
        total = [[None] * 5 for c in range(2)]
        for k in range(1, 5):
            for c in range(2):
                at = 8 + 8 * c
                flux = pair_flux(
                    left[c],
                    [ref[f, line, at + k : at + 8 + k, :] for f in range(FIELDS)],
                    direction,
                    inner[k - 1] if c == 1 else FACTORS[k - 1],
                )
                for f in range(5):
                    line_flux[u, k - 1, f, at : at + 8, :] = flux[f]
                    total[c][f] = flux[f] if k == 1 else total[c][f] + flux[f]
            for c in range(2):
                at = 8 + 8 * c
                for f in range(5):
                    total[c][f] = total[c][f] - line_flux[u, k - 1, f, at - k : at + 8 - k, :]
        return total

    def line_boundary(ref, line, direction):
        first_rows = [ref[f, line, 8:16, :] for f in range(FIELDS)]
        last_rows = [ref[f, line, 16:24, :] for f in range(FIELDS)]
        total = [None] * 5
        for k in range(1, 5):
            flux = pair_flux(
                [
                    jnp.where(is_low, ref[f, line, 8 - k : 16 - k, :], last_rows[f])
                    for f in range(FIELDS)
                ],
                [
                    jnp.where(is_low, first_rows[f], ref[f, line, 16 + k : 24 + k, :])
                    for f in range(FIELDS)
                ],
                direction,
                outer[k - 1],
            )
            for f in range(5):
                total[f] = flux[f] if k == 1 else total[f] + flux[f]
        return [jnp.where(is_low, t, 0.0) for t in total], [jnp.where(is_low, 0.0, t) for t in total]

    def plane_pair(y, k, zt):
        rows = slice(8 + 8 * zt, 16 + 8 * zt)
        return pair_flux(
            [tra[f, y + 4, rows, :] for f in range(FIELDS)],
            [tra[f, y + 4 + k, rows, :] for f in range(FIELDS)],
            1,
            FACTORS[k - 1],
        )

    def ahead(y, offsets):
        for zt in range(2):
            rows = slice(8 * zt, 8 * zt + 8)
            total = [None] * 5
            for k in offsets:
                flux = plane_pair(y, k, zt)
                for f in range(5):
                    plane_flux[k - 1, f, y + 4, rows, :] = flux[f]
                    total[f] = flux[f] if total[f] is None else total[f] + flux[f]
            for f in range(5):
                tend_t[f, y, rows, :] = total[f]

    def second_interior(y, carry):
        ahead(y, range(1, 5))
        return carry

    lax.fori_loop(0, EDGE - 4, second_interior, 0)
    for y in range(EDGE - 4, EDGE - 1):
        ahead(y, range(1, EDGE - y))
    for f in range(5):
        tend_t[f, EDGE - 1, :, :] = jnp.zeros((EDGE, LANES), jnp.float32)

    peak[1] = gather_peaks(0, 0, block_copies)
    z_copies = exchange_peaks(1, owners - 1, z_peers)

    def behind(y, offsets):
        for zt in range(2):
            rows = slice(8 * zt, 8 * zt + 8)
            for f in range(5):
                total = tend_t[f, y, rows, :]
                for k in offsets:
                    total = total - plane_flux[k - 1, f, y + 4 - k, rows, :]
                tend_t[f, y, rows, :] = total

    def second_behind(y, carry):
        behind(y, range(1, 5))
        return carry

    for y in range(1, 4):
        behind(y, range(1, y + 1))
    lax.fori_loop(4, EDGE, second_behind, 0)

    def third_line(i, carry):
        for u in range(INNER):
            y = INNER * i + u
            total = line_interior(tra, y + 4, 2, u)
            for f in range(5):
                for c in range(2):
                    rows = slice(8 * c, 8 * c + 8)
                    tend_t[f, y, rows, :] = tend_t[f, y, rows, :] + total[c][f]
        return carry

    def first_line(i, carry):
        for u in range(INNER):
            line = INNER * i + u
            total = line_interior(nat, line, 0, u)
            for f in range(5):
                for c in range(2):
                    tend_x[f, line, 8 * c : 8 * c + 8, :] = total[c][f]
        return carry

    lax.fori_loop(0, EDGE // INNER, third_line, 0)
    lax.fori_loop(0, CAP // INNER, first_line, 0)
    peak[2] = gather_peaks(1, owners - 1, z_copies)
    y_copies = exchange_peaks(2, owners + 2, y_peers)
    lax.fori_loop(CAP // INNER, 2 * CAP // INNER, first_line, 0)

    copies[0].wait_recv()
    copies[1].wait_recv()

    def third_halo(group, carry):
        for i in [4 * group + u for u in range(4)]:
            rows = pl.ds(pl.multiple_of(8 * i, 8), 8)
            lower, upper = [], []
            for f in range(5):
                below = jnp.where(lane_slot == owned_below - 1, halo_z[0, f, rows, :], 0.0)
                above = jnp.where(lane_slot == 0, halo_z[1, f, rows, :], 0.0)
                for shift in (16, 32, 64):
                    below = below + pltpu.roll(below, shift, 1)
                    above = above + pltpu.roll(above, shift, 1)
                lower.append(
                    jnp.where(lane_slot == 0, below, pltpu.roll(pack_z[1, f, rows, :], EDGE, 1))
                )
                upper.append(
                    jnp.where(
                        lane_slot == owned - 1, above, pltpu.roll(pack_z[0, f, rows, :], LANES - EDGE, 1)
                    )
                )
            lower, _ = cell_fields(lower)
            upper, _ = cell_fields(upper)
            for f in range(FIELDS):
                for j in range(2):
                    tra[f, 2 * i + j + 4, 4:8, :] = lower[f][4 * j : 4 * j + 4]
                    tra[f, 2 * i + j + 4, 24:28, :] = upper[f][4 * j : 4 * j + 4]
        return carry

    lax.fori_loop(0, (EDGE // 2) // 4, third_halo, 0)

    def third_boundary(i, carry):
        for u in range(OUTER):
            y = OUTER * i + u
            total = line_boundary(tra, y + 4, 2)
            for f in range(5):
                for c in range(2):
                    rows = slice(8 * c, 8 * c + 8)
                    tend_t[f, y, rows, :] = tend_t[f, y, rows, :] + total[c][f]
        return carry

    lax.fori_loop(0, EDGE // OUTER, third_boundary, 0)
    copies[2].wait_recv()
    copies[3].wait_recv()

    def first_halo(group, carry):
        for i in [2 * group + u for u in range(2)]:
            rows = pl.ds(pl.multiple_of(8 * i, 8), 8)
            for side in range(2):
                at = 4 if side == 0 else 24
                for half in range(2):
                    lanes = slice(half * LANES, (half + 1) * LANES)
                    fields, _ = cell_fields([halo_x[side, f, rows, lanes] for f in range(5)])
                    for f in range(FIELDS):
                        for j in range(2):
                            nat[f, 2 * (2 * i + j) + half, at : at + 4, :] = fields[f][4 * j : 4 * j + 4]
        return carry

    lax.fori_loop(0, (CAP // 2) // 2, first_halo, 0)

    def first_boundary(i, carry):
        for u in range(OUTER):
            line = OUTER * i + u
            total = line_boundary(nat, line, 0)
            for f in range(5):
                for c in range(2):
                    rows = slice(8 * c, 8 * c + 8)
                    tend_x[f, line, rows, :] = tend_x[f, line, rows, :] + total[c][f]
        return carry

    lax.fori_loop(0, 2 * CAP // OUTER, first_boundary, 0)
    for f in range(5):
        for half in range(2):
            part = tend_t[f, half * 8 : (half + 1) * 8, :, :].reshape(LANES, LANES).T
            for s in range(CAP):
                value = part[s * EDGE : (s + 1) * EDGE] + tend_x[f, 2 * s + half, :, :]
                out_ref[s, f, :, half * LANES : (half + 1) * LANES] = (
                    2.0 * value if f == 4 else value
                )
    copies[4].wait_recv()
    copies[5].wait_recv()

    def second_halo(group, carry):
        for y in [2 * group + u for u in range(2)]:
            for side in range(2):
                for zt in range(2):
                    rows = slice(8 * zt, 8 * zt + 8)
                    fields, _ = cell_fields([halo_y[side, f, y, rows, :] for f in range(5)])
                    for f in range(FIELDS):
                        tra[f, y + 20 * side, 8 + 8 * zt : 16 + 8 * zt, :] = fields[f]
        return carry

    lax.fori_loop(0, (4) // 2, second_halo, 0)
    for y in range(4):
        for zt in range(2):
            rows = slice(8 * zt, 8 * zt + 8)
            low, high = [None] * 5, [None] * 5
            for k in range(y + 1, 5):
                flux = plane_pair(y - k, k, zt)
                low = [-flux[f] if low[f] is None else low[f] - flux[f] for f in range(5)]
            for k in range(4 - y, 5):
                flux = plane_pair(y + EDGE - 4, k, zt)
                high = [flux[f] if high[f] is None else high[f] + flux[f] for f in range(5)]
            for f in range(5):
                edge_t[f, y, rows, :] = low[f]
                edge_t[f, y + 4, rows, :] = high[f]

    left_lanes = lax.broadcasted_iota(jnp.int32, (EDGE, LANES), 1) < LANES // 2
    for f in range(5):
        part = edge_t[f].reshape(LANES, LANES).T
        for s in range(CAP):
            value = part[s * EDGE : (s + 1) * EDGE]
            if f == 4:
                value = 2.0 * value
            for half in range(2):
                lanes = slice(half * LANES, (half + 1) * LANES)
                mine = left_lanes if half == 0 else jnp.logical_not(left_lanes)
                out_ref[s, f, :, lanes] = out_ref[s, f, :, lanes] + jnp.where(mine, value, 0.0)
    info_ref[1] = jnp.full((8, LANES), owned, jnp.int32).astype(jnp.float32)
    info_ref[0] = gather_peaks(2, owners + 2, y_copies)
    for copy in copies.values():
        copy.wait_send()
    reg_load.wait()


def update_kernel(tend_ref, info_ref, sol_ref, reg_ref, sol_hbm, reg_hbm, new_sol, new_reg, sems):
    fastest = jnp.max(info_ref[0], axis=(0, 1), keepdims=True)
    time_step = jnp.broadcast_to(COURANT / (EDGE * fastest), (EDGE, 2 * LANES))
    owned = jnp.broadcast_to(info_ref[1, 0:1, 0:1], (EDGE, 2 * LANES))
    copies = []
    for s in range(CAP):
        keep = owned > float(s)
        for f in range(5):
            register = LOW_STORAGE_A[SECTION] * reg_ref[s, f] + time_step * tend_ref[s, f]
            state = sol_ref[s, f] + LOW_STORAGE_B[SECTION] * register
            new_reg[s, f] = jnp.where(keep, register, 0.0)
            new_sol[s, f] = jnp.where(keep, state, 0.0)
        if s % 2 == 1:
            part = pl.ds(s - 1, 2)
            for i, (source, target) in enumerate(((new_reg, reg_hbm), (new_sol, sol_hbm))):
                copy = pltpu.make_async_copy(source.at[part], target.at[part], sems.at[i, s // 2])
                copy.start()
                copies.append(copy)
    for copy in copies:
        copy.wait()


def on_device(solution, register, counts):
    blocks, old_register = solution[0], register[0]
    shape = blocks.shape
    f32 = jnp.float32
    scratch = [
        pltpu.SMEM((OWNERS,), jnp.int32),
        pltpu.VMEM((5, EDGE, EDGE, LANES), f32),
        pltpu.VMEM((2, 5, 4 * CAP, 2 * LANES), f32),
        pltpu.VMEM((2, 5, 4 * EDGE, LANES), f32),
        pltpu.VMEM((2, 5, 4 * CAP, 2 * LANES), f32),
        pltpu.VMEM((2, 5, 4, EDGE, LANES), f32),
        pltpu.VMEM((2, 5, 4 * EDGE, LANES), f32),
        pltpu.VMEM((FIELDS, 2 * CAP, 32, LANES), f32),
        pltpu.VMEM((FIELDS, EDGE + 8, 32, LANES), f32),
        pltpu.VMEM((2, 4, 5, 24, LANES), f32),
        pltpu.VMEM((4, 5, EDGE + 4, EDGE, LANES), f32),
        pltpu.VMEM((5, 2 * CAP, EDGE, LANES), f32),
        pltpu.VMEM((5, EDGE, EDGE, LANES), f32),
        pltpu.VMEM((5, 8, EDGE, LANES), f32),
        pltpu.VMEM((3, 8, LANES), f32),
        pltpu.VMEM((13, 8, LANES), f32),
        pltpu.SemaphoreType.DMA((CAP,)),
        pltpu.SemaphoreType.DMA,
        pltpu.SemaphoreType.DMA,
        pltpu.SemaphoreType.DMA((6,)),
        pltpu.SemaphoreType.DMA((6,)),
        pltpu.SemaphoreType.DMA((13,)),
        pltpu.SemaphoreType.DMA((13,)),
    ]
    cells = jax.ShapeDtypeStruct(shape, f32)
    tendency, info, state, past = pl.pallas_call(
        tendency_kernel,
        out_shape=[cells, jax.ShapeDtypeStruct((2, 8, LANES), f32), cells, cells],
        in_specs=[pl.BlockSpec(memory_space=pltpu.HBM)] * 3,
        out_specs=[pl.BlockSpec(memory_space=pltpu.VMEM)] * 4,
        scratch_shapes=scratch,
        compiler_params=pltpu.CompilerParams(
            collective_id=0, has_side_effects=True, vmem_limit_bytes=20 * 2**20
        ),
        name="tendency",
    )(
        pltpu.with_memory_space_constraint(counts, pltpu.HBM),
        pltpu.with_memory_space_constraint(blocks, pltpu.HBM),
        pltpu.with_memory_space_constraint(old_register, pltpu.HBM),
    )
    new_solution, new_register = pl.pallas_call(
        update_kernel,
        out_shape=[jax.ShapeDtypeStruct(shape, f32)] * 2,
        in_specs=[pl.BlockSpec(memory_space=pltpu.VMEM)] * 4,
        out_specs=[pl.BlockSpec(memory_space=pltpu.HBM)] * 2,
        scratch_shapes=[
            pltpu.VMEM(shape, f32),
            pltpu.VMEM(shape, f32),
            pltpu.SemaphoreType.DMA((2, CAP // 2)),
        ],
        compiler_params=pltpu.CompilerParams(vmem_limit_bytes=8 * 2**20),
        name="update",
    )(tendency, info, state, past)
    return (new_solution[None], new_register[None])


def solution(mesh):
    in_specs = (P("group", "block", None, None, None), P("group", "block", None, None, None), P())
    out_specs = (P("group", "block", None, None, None), P("group", "block", None, None, None))
    return jax.shard_map(
        on_device, mesh=mesh, in_specs=in_specs, out_specs=out_specs, check_vma=False
    )
```

```python
import functools

import jax
import jax.numpy as jnp
from jax import lax
from jax.experimental import pallas as pl
from jax.experimental.pallas import tpu as pltpu
from jax.sharding import PartitionSpec as P

SECTION = 2
HEAT_RATIO = 1.4
COURANT = 0.5
SERIES_CUT = 0.0001
CENTRAL_WEIGHTS = (0.8, -0.2, 4.0 / 105.0, -1.0 / 280.0)
LOW_STORAGE_A = (
    0.0,
    -567301805773.0 / 1357537059087.0,
    -2404267990393.0 / 2016746695238.0,
    -3550918686646.0 / 2091501179385.0,
    -1275806237668.0 / 842570457699.0,
)
LOW_STORAGE_B = (
    1432997174477.0 / 9575080441755.0,
    5161836677717.0 / 13612068292357.0,
    1720146321549.0 / 2090206949498.0,
    3134564353537.0 / 4481467310338.0,
    2277821191437.0 / 14882151754819.0,
)
MESH = pl.DeviceIdType.MESH
EDGE = 16
CAP = 8
OWNERS = 8
LANES = 128
FIELDS = 8
INNER = 2
OUTER = 2


def cell_fields(state):
    density, first, second, third, energy = state
    inverse = 1.0 / density
    v1, v2, v3 = first * inverse, second * inverse, third * inverse
    pressure = (HEAT_RATIO - 1.0) * (energy - 0.5 * (first * v1 + second * v2 + third * v3))
    half_log = 0.5 * jnp.log(density)
    half_log_p = 0.5 * jnp.log(pressure)
    fields = [
        0.5 * density,
        0.5 * v1,
        0.5 * v2,
        0.5 * v3,
        0.5 * pressure,
        half_log,
        (HEAT_RATIO - 1.0) * (density / pressure),
        half_log - half_log_p,
    ]
    return fields, (v1, v2, v3, pressure, inverse)


def mean_parts(left, right, left_log, right_log):
    total = left + right
    step = right - left
    ratio = step / total
    ratio_sq = ratio * ratio
    near = ratio_sq < SERIES_CUT
    series = 1.0 + ratio_sq * (1.0 / 3.0 + ratio_sq * (1.0 / 5.0 + ratio_sq * (1.0 / 7.0)))
    return jnp.where(near, total, step), jnp.where(near, series, right_log - left_log)


def pair_flux(left, right, direction, factor):
    means = [left[1 + m] + right[1 + m] for m in range(3)]
    products = left[1] * right[1] + left[2] * right[2] + left[3] * right[3]
    top, bottom = mean_parts(left[0], right[0], left[5], right[5])
    top_t, bottom_t = mean_parts(left[6], right[6], left[7], right[7])
    mass = (top / bottom) * (factor * means[direction])
    inverse_mean = bottom_t / top_t
    momenta = [mass * means[m] for m in range(3)]
    momenta[direction] = momenta[direction] + factor * (left[4] + right[4])
    cross = left[4] * right[1 + direction] + right[4] * left[1 + direction]
    energy = mass * (products + inverse_mean) + factor * cross
    return [mass] + momenta + [energy]


FACTORS = tuple(-float(EDGE) * 2.0 * weight for weight in CENTRAL_WEIGHTS)


def tendency_kernel(
    counts_hbm,
    sol_hbm,
    reg_hbm,
    out_ref,
    info_ref,
    sol,
    reg,
    counts_ref,
    cons,
    pack_x,
    pack_z,
    halo_x,
    halo_y,
    halo_z,
    nat,
    tra,
    line_flux,
    plane_flux,
    tend_x,
    tend_t,
    edge_t,
    peak,
    peak_in,
    load_sem,
    counts_sem,
    reg_sem,
    send_sem,
    recv_sem,
    peak_send,
    peak_recv,
):
    g = lax.axis_index("group")
    b = lax.axis_index("block")
    groups = lax.axis_size("group")
    owners = lax.axis_size("block")
    shear = groups // 4
    zdim = groups // shear
    base = (g // zdim) * zdim
    block_peers = [(g, lax.rem(b + j, owners)) for j in range(1, owners)]
    y_peers = [(lax.rem(g + shear * j, groups), b) for j in range(1, 4)]
    z_peers = [(base + lax.rem(g - base + j, zdim), b) for j in range(1, zdim)]
    up_y, down_y = (lax.rem(g + 1, groups), b), (lax.rem(g + groups - 1, groups), b)
    up_x, down_x = y_peers[0], y_peers[2]
    up_z, down_z = block_peers[0], block_peers[-1]

    counts_load = pltpu.make_async_copy(counts_hbm, counts_ref, counts_sem)
    counts_load.start()
    loads = [pltpu.make_async_copy(sol_hbm.at[s], sol.at[s], load_sem.at[s]) for s in range(CAP)]
    for load in loads:
        load.start()
    barrier = pltpu.get_barrier_semaphore()
    everyone = [up_y, down_y] + y_peers + z_peers + block_peers
    for peer in everyone:
        pl.semaphore_signal(barrier, inc=1, device_id=peer, device_id_type=MESH)
    reg_load = pltpu.make_async_copy(reg_hbm, reg, reg_sem)
    reg_load.start()
    counts_load.wait()
    owned = counts_ref[b]
    owned_below = counts_ref[lax.rem(b + owners - 1, owners)]
    lane_slot = lax.broadcasted_iota(jnp.int32, (8, LANES), 1) // EDGE

    def natural_fields(s, fastest):
        pltpu.make_async_copy(sol_hbm.at[s], sol.at[s], load_sem.at[s]).wait()
        used = jnp.full((8, LANES), s, jnp.int32) < owned
        for half in range(2):
            for rt in range(2):
                fields, (v1, v2, v3, pressure, inverse) = cell_fields(
                    [
                        sol[s, f, 8 * rt : 8 * rt + 8, half * LANES : (half + 1) * LANES]
                        for f in range(5)
                    ]
                )
                for f in range(FIELDS):
                    nat[f, 2 * s + half, 8 + 8 * rt : 16 + 8 * rt, :] = fields[f]
                    if rt == 1:
                        nat[f, 2 * s + half, 24:32, :] = fields[f]
                speed = jnp.sqrt(v1 * v1 + v2 * v2 + v3 * v3) + jnp.sqrt(
                    HEAT_RATIO * pressure * inverse
                )
                fastest = jnp.maximum(fastest, jnp.where(used, speed, 0.0))
        return fastest

    peak[0] = lax.fori_loop(0, CAP, natural_fields, jnp.zeros((8, LANES), jnp.float32))

    for f in range(5):
        for s in range(CAP):
            pack_x[0, f, 4 * s : 4 * s + 4, :] = sol[s, f, 0:4, :]
            pack_x[1, f, 4 * s : 4 * s + 4, :] = sol[s, f, EDGE - 4 : EDGE, :]
    for f in range(5):
        for half in range(2):
            part = sol[:, f, :, half * LANES : (half + 1) * LANES].reshape(LANES, LANES)
            cons[f, half * 8 : (half + 1) * 8, :, :] = part.T.reshape(8, EDGE, LANES)
    for f in range(5):
        for y in range(EDGE):
            pack_z[0, f, 4 * y : 4 * y + 4, :] = cons[f, y, 0:4, :]
            pack_z[1, f, 4 * y : 4 * y + 4, :] = cons[f, y, EDGE - 4 : EDGE, :]

    def exchange_peaks(stage, first, peers):
        started = []
        for j, peer in enumerate(peers):
            copy = pltpu.make_async_remote_copy(
                src_ref=peak.at[stage],
                dst_ref=peak_in.at[first + j],
                send_sem=peak_send.at[first + j],
                recv_sem=peak_recv.at[first + j],
                device_id=peer,
                device_id_type=MESH,
            )
            copy.start()
            started.append(copy)
        return started

    def gather_peaks(stage, first, started):
        value = peak[stage]
        for j, copy in enumerate(started):
            copy.wait()
            value = jnp.maximum(value, peak_in[first + j])
        return value

    def send(index, source, target, peer):
        copy = pltpu.make_async_remote_copy(
            src_ref=source,
            dst_ref=target,
            send_sem=send_sem.at[index],
            recv_sem=recv_sem.at[index],
            device_id=peer,
            device_id_type=MESH,
        )
        copy.start()
        return copy

    pl.semaphore_wait(barrier, len(everyone))
    copies = {
        4: send(4, cons.at[:, EDGE - 4 : EDGE], halo_y.at[0], up_y),
        5: send(5, cons.at[:, 0:4], halo_y.at[1], down_y),
    }
    block_copies = exchange_peaks(0, 0, block_peers)
    copies[2] = send(2, pack_x.at[1], halo_x.at[0], up_x)
    copies[3] = send(3, pack_x.at[0], halo_x.at[1], down_x)
    copies[0] = send(0, pack_z.at[1], halo_z.at[0], up_z)
    copies[1] = send(1, pack_z.at[0], halo_z.at[1], down_z)

    def transposed_fields(group, carry):
        for y in [2 * group + u for u in range(2)]:
            for zt in range(2):
                rows = slice(8 * zt, 8 * zt + 8)
                fields = cell_fields([cons[f, y, rows, :] for f in range(5)])[0]
                for f in range(FIELDS):
                    tra[f, y + 4, 8 + 8 * zt : 16 + 8 * zt, :] = fields[f]
                    if zt == 1:
                        tra[f, y + 4, 24:32, :] = fields[f]
        return carry

    lax.fori_loop(0, (EDGE) // 2, transposed_fields, 0)


    row = lax.broadcasted_iota(jnp.int32, (8, LANES), 0)
    is_low = row < 4
    inner = [jnp.where(row < 8 - k, FACTORS[k - 1], 0.0) for k in range(1, 5)]
    outer = [
        jnp.where(
            is_low,
            jnp.where(row < k, -FACTORS[k - 1], 0.0),
            jnp.where(row >= 8 - k, FACTORS[k - 1], 0.0),
        )
        for k in range(1, 5)
    ]
    for u in range(2):
        for k in range(4):
            for f in range(5):
                line_flux[u, k, f, 0:8, :] = jnp.zeros((8, LANES), jnp.float32)

    def line_interior(ref, line, direction, u):
        left = [
            [ref[f, line, 8 + 8 * c : 16 + 8 * c, :] for f in range(FIELDS)] for c in range(2)
        ]
        total = [[None] * 5 for c in range(2)]
        for k in range(1, 5):
            for c in range(2):
                at = 8 + 8 * c
                flux = pair_flux(
                    left[c],
                    [ref[f, line, at + k : at + 8 + k, :] for f in range(FIELDS)],
                    direction,
                    inner[k - 1] if c == 1 else FACTORS[k - 1],
                )
                for f in range(5):
                    line_flux[u, k - 1, f, at : at + 8, :] = flux[f]
                    total[c][f] = flux[f] if k == 1 else total[c][f] + flux[f]
            for c in range(2):
                at = 8 + 8 * c
                for f in range(5):
                    total[c][f] = total[c][f] - line_flux[u, k - 1, f, at - k : at + 8 - k, :]
        return total

    def line_boundary(ref, line, direction):
        first_rows = [ref[f, line, 8:16, :] for f in range(FIELDS)]
        last_rows = [ref[f, line, 16:24, :] for f in range(FIELDS)]
        total = [None] * 5
        for k in range(1, 5):
            flux = pair_flux(
                [
                    jnp.where(is_low, ref[f, line, 8 - k : 16 - k, :], last_rows[f])
                    for f in range(FIELDS)
                ],
                [
                    jnp.where(is_low, first_rows[f], ref[f, line, 16 + k : 24 + k, :])
                    for f in range(FIELDS)
                ],
                direction,
                outer[k - 1],
            )
            for f in range(5):
                total[f] = flux[f] if k == 1 else total[f] + flux[f]
        return [jnp.where(is_low, t, 0.0) for t in total], [jnp.where(is_low, 0.0, t) for t in total]

    def plane_pair(y, k, zt):
        rows = slice(8 + 8 * zt, 16 + 8 * zt)
        return pair_flux(
            [tra[f, y + 4, rows, :] for f in range(FIELDS)],
            [tra[f, y + 4 + k, rows, :] for f in range(FIELDS)],
            1,
            FACTORS[k - 1],
        )

    def ahead(y, offsets):
        for zt in range(2):
            rows = slice(8 * zt, 8 * zt + 8)
            total = [None] * 5
            for k in offsets:
                flux = plane_pair(y, k, zt)
                for f in range(5):
                    plane_flux[k - 1, f, y + 4, rows, :] = flux[f]
                    total[f] = flux[f] if total[f] is None else total[f] + flux[f]
            for f in range(5):
                tend_t[f, y, rows, :] = total[f]

    def second_interior(y, carry):
        ahead(y, range(1, 5))
        return carry

    lax.fori_loop(0, EDGE - 4, second_interior, 0)
    for y in range(EDGE - 4, EDGE - 1):
        ahead(y, range(1, EDGE - y))
    for f in range(5):
        tend_t[f, EDGE - 1, :, :] = jnp.zeros((EDGE, LANES), jnp.float32)

    def behind(y, offsets):
        for zt in range(2):
            rows = slice(8 * zt, 8 * zt + 8)
            for f in range(5):
                total = tend_t[f, y, rows, :]
                for k in offsets:
                    total = total - plane_flux[k - 1, f, y + 4 - k, rows, :]
                tend_t[f, y, rows, :] = total

    def second_behind(y, carry):
        behind(y, range(1, 5))
        return carry

    for y in range(1, 4):
        behind(y, range(1, y + 1))
    lax.fori_loop(4, EDGE, second_behind, 0)

    peak[1] = gather_peaks(0, 0, block_copies)
    z_copies = exchange_peaks(1, owners - 1, z_peers)

    def third_line(i, carry):
        for u in range(INNER):
            y = INNER * i + u
            total = line_interior(tra, y + 4, 2, u)
            for f in range(5):
                for c in range(2):
                    rows = slice(8 * c, 8 * c + 8)
                    tend_t[f, y, rows, :] = tend_t[f, y, rows, :] + total[c][f]
        return carry

    def first_line(i, carry):
        for u in range(INNER):
            line = INNER * i + u
            total = line_interior(nat, line, 0, u)
            for f in range(5):
                for c in range(2):
                    tend_x[f, line, 8 * c : 8 * c + 8, :] = total[c][f]
        return carry

    lax.fori_loop(0, EDGE // INNER, third_line, 0)
    lax.fori_loop(0, CAP // INNER, first_line, 0)
    peak[2] = gather_peaks(1, owners - 1, z_copies)
    y_copies = exchange_peaks(2, owners + 2, y_peers)
    lax.fori_loop(CAP // INNER, 2 * CAP // INNER, first_line, 0)

    copies[0].wait_recv()
    copies[1].wait_recv()

    def third_halo(group, carry):
        for i in [4 * group + u for u in range(4)]:
            rows = pl.ds(pl.multiple_of(8 * i, 8), 8)
            lower, upper = [], []
            for f in range(5):
                below = jnp.where(lane_slot == owned_below - 1, halo_z[0, f, rows, :], 0.0)
                above = jnp.where(lane_slot == 0, halo_z[1, f, rows, :], 0.0)
                for shift in (16, 32, 64):
                    below = below + pltpu.roll(below, shift, 1)
                    above = above + pltpu.roll(above, shift, 1)
                lower.append(
                    jnp.where(lane_slot == 0, below, pltpu.roll(pack_z[1, f, rows, :], EDGE, 1))
                )
                upper.append(
                    jnp.where(
                        lane_slot == owned - 1, above, pltpu.roll(pack_z[0, f, rows, :], LANES - EDGE, 1)
                    )
                )
            lower, _ = cell_fields(lower)
            upper, _ = cell_fields(upper)
            for f in range(FIELDS):
                for j in range(2):
                    tra[f, 2 * i + j + 4, 4:8, :] = lower[f][4 * j : 4 * j + 4]
                    tra[f, 2 * i + j + 4, 24:28, :] = upper[f][4 * j : 4 * j + 4]
        return carry

    lax.fori_loop(0, (EDGE // 2) // 4, third_halo, 0)

    def third_boundary(i, carry):
        for u in range(OUTER):
            y = OUTER * i + u
            total = line_boundary(tra, y + 4, 2)
            for f in range(5):
                for c in range(2):
                    rows = slice(8 * c, 8 * c + 8)
                    tend_t[f, y, rows, :] = tend_t[f, y, rows, :] + total[c][f]
        return carry

    lax.fori_loop(0, EDGE // OUTER, third_boundary, 0)
    copies[2].wait_recv()
    copies[3].wait_recv()

    def first_halo(group, carry):
        for i in [2 * group + u for u in range(2)]:
            rows = pl.ds(pl.multiple_of(8 * i, 8), 8)
            for side in range(2):
                at = 4 if side == 0 else 24
                for half in range(2):
                    lanes = slice(half * LANES, (half + 1) * LANES)
                    fields, _ = cell_fields([halo_x[side, f, rows, lanes] for f in range(5)])
                    for f in range(FIELDS):
                        for j in range(2):
                            nat[f, 2 * (2 * i + j) + half, at : at + 4, :] = fields[f][4 * j : 4 * j + 4]
        return carry

    lax.fori_loop(0, (CAP // 2) // 2, first_halo, 0)

    def first_boundary(i, carry):
        for u in range(OUTER):
            line = OUTER * i + u
            total = line_boundary(nat, line, 0)
            for f in range(5):
                for c in range(2):
                    rows = slice(8 * c, 8 * c + 8)
                    tend_x[f, line, rows, :] = tend_x[f, line, rows, :] + total[c][f]
        return carry

    lax.fori_loop(0, 2 * CAP // OUTER, first_boundary, 0)
    for f in range(5):
        for half in range(2):
            part = tend_t[f, half * 8 : (half + 1) * 8, :, :].reshape(LANES, LANES).T
            for s in range(CAP):
                value = part[s * EDGE : (s + 1) * EDGE] + tend_x[f, 2 * s + half, :, :]
                out_ref[s, f, :, half * LANES : (half + 1) * LANES] = (
                    2.0 * value if f == 4 else value
                )
    copies[4].wait_recv()
    copies[5].wait_recv()

    def second_halo(group, carry):
        for y in [2 * group + u for u in range(2)]:
            for side in range(2):
                for zt in range(2):
                    rows = slice(8 * zt, 8 * zt + 8)
                    fields, _ = cell_fields([halo_y[side, f, y, rows, :] for f in range(5)])
                    for f in range(FIELDS):
                        tra[f, y + 20 * side, 8 + 8 * zt : 16 + 8 * zt, :] = fields[f]
        return carry

    lax.fori_loop(0, (4) // 2, second_halo, 0)
    for y in range(4):
        for zt in range(2):
            rows = slice(8 * zt, 8 * zt + 8)
            low, high = [None] * 5, [None] * 5
            for k in range(y + 1, 5):
                flux = plane_pair(y - k, k, zt)
                low = [-flux[f] if low[f] is None else low[f] - flux[f] for f in range(5)]
            for k in range(4 - y, 5):
                flux = plane_pair(y + EDGE - 4, k, zt)
                high = [flux[f] if high[f] is None else high[f] + flux[f] for f in range(5)]
            for f in range(5):
                edge_t[f, y, rows, :] = low[f]
                edge_t[f, y + 4, rows, :] = high[f]

    left_lanes = lax.broadcasted_iota(jnp.int32, (EDGE, LANES), 1) < LANES // 2
    for f in range(5):
        part = edge_t[f].reshape(LANES, LANES).T
        for s in range(CAP):
            value = part[s * EDGE : (s + 1) * EDGE]
            if f == 4:
                value = 2.0 * value
            for half in range(2):
                lanes = slice(half * LANES, (half + 1) * LANES)
                mine = left_lanes if half == 0 else jnp.logical_not(left_lanes)
                out_ref[s, f, :, lanes] = out_ref[s, f, :, lanes] + jnp.where(mine, value, 0.0)
    info_ref[1] = jnp.full((8, LANES), owned, jnp.int32).astype(jnp.float32)
    info_ref[0] = gather_peaks(2, owners + 2, y_copies)
    for copy in copies.values():
        copy.wait_send()
    reg_load.wait()


def update_kernel(tend_ref, info_ref, sol_ref, reg_ref, sol_hbm, reg_hbm, new_sol, new_reg, sems):
    fastest = jnp.max(info_ref[0], axis=(0, 1), keepdims=True)
    time_step = jnp.broadcast_to(COURANT / (EDGE * fastest), (EDGE, 2 * LANES))
    owned = jnp.broadcast_to(info_ref[1, 0:1, 0:1], (EDGE, 2 * LANES))
    copies = []
    for s in range(CAP):
        keep = owned > float(s)
        for f in range(5):
            register = LOW_STORAGE_A[SECTION] * reg_ref[s, f] + time_step * tend_ref[s, f]
            state = sol_ref[s, f] + LOW_STORAGE_B[SECTION] * register
            new_reg[s, f] = jnp.where(keep, register, 0.0)
            new_sol[s, f] = jnp.where(keep, state, 0.0)
        if s % 2 == 1:
            part = pl.ds(s - 1, 2)
            for i, (source, target) in enumerate(((new_reg, reg_hbm), (new_sol, sol_hbm))):
                copy = pltpu.make_async_copy(source.at[part], target.at[part], sems.at[i, s // 2])
                copy.start()
                copies.append(copy)
    for copy in copies:
        copy.wait()


def on_device(solution, register, counts):
    blocks, old_register = solution[0], register[0]
    shape = blocks.shape
    f32 = jnp.float32
    scratch = [
        pltpu.SMEM((OWNERS,), jnp.int32),
        pltpu.VMEM((5, EDGE, EDGE, LANES), f32),
        pltpu.VMEM((2, 5, 4 * CAP, 2 * LANES), f32),
        pltpu.VMEM((2, 5, 4 * EDGE, LANES), f32),
        pltpu.VMEM((2, 5, 4 * CAP, 2 * LANES), f32),
        pltpu.VMEM((2, 5, 4, EDGE, LANES), f32),
        pltpu.VMEM((2, 5, 4 * EDGE, LANES), f32),
        pltpu.VMEM((FIELDS, 2 * CAP, 32, LANES), f32),
        pltpu.VMEM((FIELDS, EDGE + 8, 32, LANES), f32),
        pltpu.VMEM((2, 4, 5, 24, LANES), f32),
        pltpu.VMEM((4, 5, EDGE + 4, EDGE, LANES), f32),
        pltpu.VMEM((5, 2 * CAP, EDGE, LANES), f32),
        pltpu.VMEM((5, EDGE, EDGE, LANES), f32),
        pltpu.VMEM((5, 8, EDGE, LANES), f32),
        pltpu.VMEM((3, 8, LANES), f32),
        pltpu.VMEM((13, 8, LANES), f32),
        pltpu.SemaphoreType.DMA((CAP,)),
        pltpu.SemaphoreType.DMA,
        pltpu.SemaphoreType.DMA,
        pltpu.SemaphoreType.DMA((6,)),
        pltpu.SemaphoreType.DMA((6,)),
        pltpu.SemaphoreType.DMA((13,)),
        pltpu.SemaphoreType.DMA((13,)),
    ]
    cells = jax.ShapeDtypeStruct(shape, f32)
    tendency, info, state, past = pl.pallas_call(
        tendency_kernel,
        out_shape=[cells, jax.ShapeDtypeStruct((2, 8, LANES), f32), cells, cells],
        in_specs=[pl.BlockSpec(memory_space=pltpu.HBM)] * 3,
        out_specs=[pl.BlockSpec(memory_space=pltpu.VMEM)] * 4,
        scratch_shapes=scratch,
        compiler_params=pltpu.CompilerParams(
            collective_id=0, has_side_effects=True, vmem_limit_bytes=20 * 2**20
        ),
        name="tendency",
    )(
        pltpu.with_memory_space_constraint(counts, pltpu.HBM),
        pltpu.with_memory_space_constraint(blocks, pltpu.HBM),
        pltpu.with_memory_space_constraint(old_register, pltpu.HBM),
    )
    new_solution, new_register = pl.pallas_call(
        update_kernel,
        out_shape=[jax.ShapeDtypeStruct(shape, f32)] * 2,
        in_specs=[pl.BlockSpec(memory_space=pltpu.VMEM)] * 4,
        out_specs=[pl.BlockSpec(memory_space=pltpu.HBM)] * 2,
        scratch_shapes=[
            pltpu.VMEM(shape, f32),
            pltpu.VMEM(shape, f32),
            pltpu.SemaphoreType.DMA((2, CAP // 2)),
        ],
        compiler_params=pltpu.CompilerParams(vmem_limit_bytes=8 * 2**20),
        name="update",
    )(tendency, info, state, past)
    return (new_solution[None], new_register[None])


def solution(mesh):
    in_specs = (P("group", "block", None, None, None), P("group", "block", None, None, None), P())
    out_specs = (P("group", "block", None, None, None), P("group", "block", None, None, None))
    return jax.shard_map(
        on_device, mesh=mesh, in_specs=in_specs, out_specs=out_specs, check_vma=False
    )
```
